512 devices in a mesh: space: 64 (over z_lo, x, y), tm: 8 (over z_hi, core).
Axes of the slice: x: 4, y: 8, z: 8 (z_hi: 4, z_lo: 2; z = z_hi * 2 + z_lo), core: 2. Of those that a mesh axis runs over, the one named last changes fastest.
Arguments:
- source: bfloat16 [16, 128, 4, 2, 3, 16, 128], P('tm', 'space'), may hold values from -6 to 6
- gauge_links: bfloat16 [16, 128, 4, 2, 3, 3, 128], P('tm', 'space'), may hold values from -2.5 to 2.5
- clover: bfloat16 [16, 128, 2, 2, 6, 6, 128], P('tm', 'space'), may hold values from -0.3984375 to 0.3984375
- eigenvectors: bfloat16 [16, 128, 2, 3, 256, 128], P('tm', 'space'), may hold values from -4 to 4
- elemental: bfloat16 [16, 2, 256, 256], P('tm'), may hold values from -0.25 to 0.25
Outputs:
- sink_field: bfloat16 [16, 128, 4, 2, 3, 16, 128], P('tm', 'space')
The draws below stay inside these ranges and needn't reach their ends.
All inputs are finite; a program needn't handle non-finite values.
Results may differ from the reference program's by a relative error of at most 0.0057.
Values may be sent and summed in bfloat16 or wider, within the bound.
No kernel may reach another device: no remote copies, remote signals or barrier semaphores. Data moves between devices by JAX's collectives and lax.ppermute only.
A program may use at most 64 MiB of HBM per device.

```python
import jax
import jax.numpy as jnp
import numpy as np
from jax import lax

X = 16
Y = 8
COLS = 16
NEV = 256
NZ = 128
NT = 16


def block_scale(stream_key, extent, shards, smallest, top_value):
    factor_of, own = 1.0, jax.random.fold_in(stream_key, 6)
    for position, blocks in shards:
        steps = jnp.exp(jax.random.uniform(jax.random.fold_in(own, position), (blocks,), jnp.float32, smallest / len(shards), top_value / len(shards)))
        factor_of = factor_of * jnp.repeat(steps, extent[position] // blocks).reshape([-1 if axis == position else 1 for axis in range(len(extent))])
    return factor_of


def normal_values(key, extent, scale, most, shards=(), held_as=jnp.bfloat16):
    array = scale * jax.random.normal(key, extent, jnp.float32)
    if shards:
        array = array * block_scale(key, extent, shards, -0.22, 0.18)
    return jnp.clip(array, -most, most).astype(held_as)


def setup_inputs(seed: int = 0) -> dict:
    streams_of = jax.random.split(jax.random.key(seed), 6)
    return {
        "source": normal_values(streams_of[0], (NT, NZ, 4, 2, 3, COLS, X * Y), 1.0, 6.0, ((0, 8), (1, 64))),
        "gauge_links": normal_values(streams_of[1], (NT, NZ, 4, 2, 3, 3, X * Y), 6 ** -0.5, 2.5, ((0, 8), (1, 64))),
        "clover": normal_values(streams_of[2], (NT, NZ, 2, 2, 6, 6, X * Y), 0.06, 0.3984375, ((0, 8), (1, 64))),
        "eigenvectors": normal_values(streams_of[3], (NT, NZ, 2, 3, NEV, X * Y), 2 ** -0.5, 4.0, ((0, 8), (1, 64))),
        "elemental": normal_values(streams_of[4], (NT, 2, NEV, NEV), (2 * NEV) ** -0.5, 0.25, ((0, 8),)),
    }


HOPPING = 0.125


def gamma_tables():
    half_real = np.zeros((4, 2, 2))
    half_imag = np.zeros((4, 2, 2))
    half_imag[0] = [[0.0, -1.0], [-1.0, 0.0]]
    half_real[1] = [[0.0, -1.0], [1.0, 0.0]]
    half_imag[2] = [[-1.0, 0.0], [0.0, 1.0]]
    half_real[3] = [[1.0, 0.0], [0.0, 1.0]]
    gamma_real = np.zeros((4, 4, 4))
    gamma_imag = np.zeros((4, 4, 4))
    gamma_real[:, 0:2, 2:4] = half_real
    gamma_real[:, 2:4, 0:2] = np.transpose(half_real, (0, 2, 1))
    gamma_imag[:, 0:2, 2:4] = half_imag
    gamma_imag[:, 2:4, 0:2] = -np.transpose(half_imag, (0, 2, 1))
    return gamma_real, gamma_imag


def spin_product(matrix_table, component):
    return jnp.einsum('pq,tq...->tp...', jnp.asarray(matrix_table, jnp.float32), component, precision=lax.Precision.HIGHEST)


def spin_times(table_real, table_imag, spinor):
    real_part = spin_product(table_real, spinor[:, :, 0]) - spin_product(table_imag, spinor[:, :, 1])
    imag_part = spin_product(table_real, spinor[:, :, 1]) + spin_product(table_imag, spinor[:, :, 0])
    return jnp.stack([real_part, imag_part], axis=2)


def colour_product(matrix, component):
    return jnp.einsum('tab...,tpb...->tpa...', matrix, component, precision=lax.Precision.HIGHEST)


def colour_times(matrix, spinor):
    real_part = colour_product(matrix[:, 0], spinor[:, :, 0]) - colour_product(matrix[:, 1], spinor[:, :, 1])
    imag_part = colour_product(matrix[:, 0], spinor[:, :, 1]) + colour_product(matrix[:, 1], spinor[:, :, 0])
    return jnp.stack([real_part, imag_part], axis=2)


def adjoint(matrix):
    return jnp.stack([jnp.swapaxes(matrix[:, 0], 1, 2), -jnp.swapaxes(matrix[:, 1], 1, 2)], axis=1)


def block_product(matrix, component):
    return jnp.einsum('tij...,tj...->ti...', matrix, component, precision=lax.Precision.HIGHEST)


def clover_times(clover, spinor):
    block_list = []
    for chiral in range(2):
        block_in = jnp.swapaxes(spinor[:, 2 * chiral:2 * chiral + 2], 1, 2)
        block_in = block_in.reshape(block_in.shape[:2] + (6,) + block_in.shape[4:])
        matrix = clover[:, chiral]
        real_part = block_product(matrix[:, 0], block_in[:, 0]) - block_product(matrix[:, 1], block_in[:, 1])
        imag_part = block_product(matrix[:, 0], block_in[:, 1]) + block_product(matrix[:, 1], block_in[:, 0])
        block_out = jnp.stack([real_part, imag_part], axis=1)
        block_out = block_out.reshape(block_out.shape[:2] + (2, 3) + block_out.shape[3:])
        block_list.append(jnp.swapaxes(block_out, 1, 2))
    return jnp.concatenate(block_list, axis=1)


def dirac_full(spinor, links, clover):
    gamma_real, gamma_imag = gamma_tables()
    identity = np.eye(4)
    slice_ids = jnp.arange(NT)
    shape_time = (NT,) + (1,) * (spinor.ndim - 1)
    last_sign = jnp.where(slice_ids == NT - 1, -1.0, 1.0).astype(jnp.float32).reshape(shape_time)
    first_sign = jnp.where(slice_ids == 0, -1.0, 1.0).astype(jnp.float32).reshape(shape_time)
    ahead_signs = (1.0, 1.0, 1.0, last_sign)
    behind_signs = (1.0, 1.0, 1.0, first_sign)
    hopping = jnp.zeros_like(spinor)
    for hop_direction in range(4):
        dimension_index = (6, 5, 4, 0)[hop_direction]
        matrix = links[:, hop_direction]
        ahead = jnp.roll(spinor, -1, dimension_index) * ahead_signs[hop_direction]
        moved = jnp.roll(colour_times(adjoint(matrix), spinor), 1, dimension_index) * behind_signs[hop_direction]
        hopping = hopping + spin_times(identity - gamma_real[hop_direction], -gamma_imag[hop_direction], colour_times(matrix, ahead))
        hopping = hopping + spin_times(identity + gamma_real[hop_direction], gamma_imag[hop_direction], moved)
    return spinor + clover_times(clover, spinor) - HOPPING * hopping


def reference(source, gauge_links, clover, eigenvectors, elemental):
    links32 = jnp.moveaxis(gauge_links.astype(jnp.float32), 1, 5).reshape(NT, 4, 2, 3, 3, NZ, Y, X)
    clover32 = jnp.moveaxis(clover.astype(jnp.float32), 1, 5).reshape(NT, 2, 2, 6, 6, NZ, Y, X)
    columns_first = jnp.moveaxis(source, 5, 0)

    def forward_column(column_in):
        spinor = jnp.moveaxis(column_in.astype(jnp.float32), 1, 4).reshape(NT, 4, 2, 3, NZ, Y, X)
        once = dirac_full(spinor, links32, clover32)
        twice = dirac_full(once, links32, clover32)
        return jnp.moveaxis(twice.astype(jnp.bfloat16).reshape(NT, 4, 2, 3, NZ, Y * X), 4, 1)

    rounded = lax.map(forward_column, columns_first)
    normaliser = (3.0 * X * Y * NZ) ** -0.5

    def slice_work(slice_index):
        basis = eigenvectors[slice_index].astype(jnp.float32)
        spinor = rounded[:, slice_index].astype(jnp.float32)
        turned = jnp.stack([spinor[:, :, :, 1], -spinor[:, :, :, 0]], axis=3)
        stacked = jnp.stack([spinor, turned], axis=3)
        coefficient = jnp.einsum('zrckq,jzpwrcq->kpjw', basis, stacked, precision=lax.Precision.HIGHEST) * normaliser
        weights = elemental[slice_index].astype(jnp.float32)
        flat_coef = coefficient.reshape(NEV, 4 * COLS, 2)
        mixed_real = jnp.dot(weights[0], flat_coef[:, :, 0], precision=lax.Precision.HIGHEST) - jnp.dot(weights[1], flat_coef[:, :, 1], precision=lax.Precision.HIGHEST)
        mixed_imag = jnp.dot(weights[0], flat_coef[:, :, 1], precision=lax.Precision.HIGHEST) + jnp.dot(weights[1], flat_coef[:, :, 0], precision=lax.Precision.HIGHEST)
        mixed_coef = jnp.stack([mixed_real, mixed_imag], axis=-1).reshape(NEV, 4, COLS, 2).astype(jnp.bfloat16)
        values_in = mixed_coef.astype(jnp.float32)

        def expand_product(left_factor, right_factor):
            return jnp.einsum('zckq,kpj->jzpcq', left_factor, right_factor, precision=lax.Precision.HIGHEST)

        real_part = expand_product(basis[:, 0], values_in[..., 0]) - expand_product(basis[:, 1], values_in[..., 1])
        imag_part = expand_product(basis[:, 0], values_in[..., 1]) + expand_product(basis[:, 1], values_in[..., 0])
        return jnp.stack([real_part, imag_part], axis=3) * NEV ** -0.5

    expanded = lax.map(slice_work, jnp.arange(NT, dtype=jnp.int32))

    def column_sink(column_number):
        spinor = jnp.moveaxis(expanded[:, column_number], 1, 4).reshape(NT, 4, 2, 3, NZ, Y, X)
        result = dirac_full(dirac_full(spinor, links32, clover32), links32, clover32)
        return jnp.moveaxis(result.astype(jnp.bfloat16).reshape(NT, 4, 2, 3, NZ, Y * X), 4, 1)

    sink_columns = lax.map(column_sink, jnp.arange(COLS, dtype=jnp.int32))
    return jnp.moveaxis(sink_columns, 0, 5)
```

```python
import jax
import jax.numpy as jnp
from jax import lax
from jax.sharding import PartitionSpec as P

X = 16
Y = 8


HOPPING = 0.125
HALF_MAP = (
    ((1, 0.0, -1.0), (0, 0.0, -1.0)),
    ((1, -1.0, 0.0), (0, 1.0, 0.0)),
    ((0, 0.0, -1.0), (1, 0.0, 1.0)),
    ((0, 1.0, 0.0), (1, 1.0, 0.0)),
)


def passed_along(value, axis, by):
    count = lax.axis_size(axis)
    return lax.ppermute(value, axis, [(i, (i + by) % count) for i in range(count)])


def dagger_map(forward_map):
    result = [None, None]
    for row_number in range(2):
        column, real_coef, imag_coef = forward_map[row_number]
        result[column] = (row_number, real_coef, -imag_coef)
    return tuple(result)


def apply_half(spin_map, half_spinor):
    outputs = []
    for column, real_coef, imag_coef in spin_map:
        picked = half_spinor[:, :, column]
        real_in = picked[:, :, 0]
        imag_in = picked[:, :, 1]
        outputs.append(
            jnp.stack(
                [
                    real_coef * real_in - imag_coef * imag_in,
                    real_coef * imag_in + imag_coef * real_in,
                ],
                axis=2,
            )
        )
    return jnp.stack(outputs, axis=2)


def project(spinor, spin_map, sign_value):
    return spinor[:, :, 0:2] + sign_value * apply_half(spin_map, spinor[:, :, 2:4])


def colour_apply(matrix, spinor):
    real_out = 0.0
    imag_out = 0.0
    for colour in range(3):
        left_real = matrix[:, :, 0, :, colour][:, :, None, :, None, :]
        left_imag = matrix[:, :, 1, :, colour][:, :, None, :, None, :]
        right_real = spinor[:, :, :, 0, colour][:, :, :, None]
        right_imag = spinor[:, :, :, 1, colour][:, :, :, None]
        real_out = real_out + left_real * right_real - left_imag * right_imag
        imag_out = imag_out + left_real * right_imag + left_imag * right_real
    return jnp.stack([real_out, imag_out], axis=3)


def adjoint(matrix):
    return jnp.stack(
        [jnp.swapaxes(matrix[:, :, 0], 2, 3), -jnp.swapaxes(matrix[:, :, 1], 2, 3)], axis=2
    )


def clover_apply(clover, spinor):
    block_list = []
    for chiral in range(2):
        clover_block = clover[:, :, chiral]
        new_shape = clover_block.shape[:2] + (2, 3, 6, clover_block.shape[-1])
        rows_real = clover_block[:, :, 0].reshape(new_shape)
        rows_imag = clover_block[:, :, 1].reshape(new_shape)
        real_out = 0.0
        imag_out = 0.0
        for source_index in range(6):
            spin_in = 2 * chiral + source_index // 3
            colour_in = source_index % 3
            left_real = rows_real[:, :, :, :, source_index][:, :, :, :, None, :]
            left_imag = rows_imag[:, :, :, :, source_index][:, :, :, :, None, :]
            right_real = spinor[:, :, spin_in, 0, colour_in][:, :, None, None]
            right_imag = spinor[:, :, spin_in, 1, colour_in][:, :, None, None]
            real_out = real_out + left_real * right_real - left_imag * right_imag
            imag_out = imag_out + left_real * right_imag + left_imag * right_real
        block_list.append(jnp.stack([real_out, imag_out], axis=3))
    return jnp.concatenate(block_list, axis=2)


def roll_plane(array_in, offset, hop_direction):
    sites = array_in.shape[-1]
    period = X if hop_direction == 0 else Y
    stride = 1 if hop_direction == 0 else X
    position = jnp.arange(sites) // stride % period
    if offset < 0:
        at_edge = position == period - 1
        wrapped = jnp.roll(array_in, (period - 1) * stride, axis=-1)
        plain = jnp.roll(array_in, -stride, axis=-1)
    else:
        at_edge = position == 0
        wrapped = jnp.roll(array_in, -(period - 1) * stride, axis=-1)
        plain = jnp.roll(array_in, stride, axis=-1)
    return jnp.where(at_edge, wrapped, plain)


def dirac(centre, links, clover, first_sign, last_sign):
    halves = {}
    for hop_direction, (axis, dim, before_sign, after_sign) in (
        (2, ("space", 1, None, None)),
        (3, ("tm", 0, first_sign, last_sign)),
    ):
        size = centre.shape[dim]
        here_links = links[:, :, hop_direction]
        forward_map = HALF_MAP[hop_direction]
        ahead_own = project(centre, forward_map, -1.0)
        behind_own = colour_apply(adjoint(here_links), project(centre, forward_map, 1.0))
        low = lax.slice_in_dim(ahead_own, 0, 1, axis=dim)
        high = lax.slice_in_dim(behind_own, size - 1, size, axis=dim)
        after = passed_along(low.astype(jnp.bfloat16), axis, -1).astype(jnp.float32)
        before = passed_along(high.astype(jnp.bfloat16), axis, 1).astype(jnp.float32)
        if after_sign is not None:
            after = after * after_sign
            before = before * before_sign
        ahead = jnp.concatenate([lax.slice_in_dim(ahead_own, 1, size, axis=dim), after], axis=dim)
        behind = jnp.concatenate(
            [before, lax.slice_in_dim(behind_own, 0, size - 1, axis=dim)], axis=dim
        )
        halves[hop_direction] = (ahead, behind)
    hopping = 0.0
    for hop_direction in range(4):
        forward_map = HALF_MAP[hop_direction]
        backward_map = dagger_map(forward_map)
        here_links = links[:, :, hop_direction]
        if hop_direction < 2:
            ahead = roll_plane(project(centre, forward_map, -1.0), -1, hop_direction)
            behind = roll_plane(
                colour_apply(adjoint(here_links), project(centre, forward_map, 1.0)),
                1,
                hop_direction,
            )
        else:
            ahead, behind = halves[hop_direction]
        forward_part = colour_apply(here_links, ahead)
        hopping = hopping + jnp.concatenate(
            [forward_part + behind, apply_half(backward_map, behind - forward_part)], axis=2
        )
    return centre + clover_apply(clover, centre) - HOPPING * hopping


def mix_coefficients(elemental, shares):
    weights = elemental.astype(jnp.float32)

    def product(component, values):
        return jnp.einsum(
            "okj,oj->ok", weights[:, component], values, precision=lax.Precision.HIGHEST
        )

    real = product(0, shares[:, 0]) - product(1, shares[:, 1])
    imag = product(0, shares[:, 1]) + product(1, shares[:, 0])
    return jnp.stack([real, imag], axis=1).astype(jnp.bfloat16)


def on_device(source, gauge_links, clover, eigenvectors, elemental):
    slices = source.shape[0]
    layers = source.shape[1]
    columns = source.shape[5]
    eigen_count = eigenvectors.shape[4]
    space_count = lax.axis_size("space")
    tm_position = lax.axis_index("tm")
    tm_count = lax.axis_size("tm")
    first_sign = jnp.where(tm_position == 0, -1.0, 1.0)
    last_sign = jnp.where(tm_position == tm_count - 1, -1.0, 1.0)
    links_f32 = gauge_links.astype(jnp.float32)
    clover_f32 = clover.astype(jnp.float32)

    def apply_twice(spinor):
        for _ in range(2):
            spinor = dirac(spinor, links_f32, clover_f32, first_sign, last_sign)
        return spinor

    rounded = apply_twice(source.astype(jnp.float32)).astype(jnp.bfloat16)
    normaliser = (3.0 * X * Y * layers * space_count) ** (-0.5)
    products = 0.0
    for colour in range(3):
        products = products + lax.dot_general(
            rounded[:, :, :, :, colour],
            eigenvectors[:, :, :, colour],
            (((1, 5), (1, 4)), ((0,), (0,))),
            preferred_element_type=jnp.float32,
        )
    real_part = products[:, :, 0, :, 0] + products[:, :, 1, :, 1]
    imag_part = products[:, :, 1, :, 0] - products[:, :, 0, :, 1]
    partial_sums = jnp.stack([real_part, imag_part], axis=3) * normaliser
    partial_sums = jnp.moveaxis(partial_sums, 0, 2).reshape(
        4 * columns, slices, 2, eigen_count
    )
    gathered = lax.all_to_all(partial_sums, "space", 0, 0, tiled=True)
    per_device = 4 * columns // space_count
    shares = gathered.reshape(space_count, per_device, slices, 2, eigen_count).sum(0)
    mixed = jnp.stack([mix_coefficients(elemental, shares[i]) for i in range(per_device)])
    everywhere = jnp.broadcast_to(mixed[None], (space_count,) + mixed.shape)
    everywhere = everywhere.reshape((space_count * per_device,) + mixed.shape[1:])
    mixed_coef = lax.all_to_all(everywhere, "space", 0, 0, tiled=True)
    parts = jnp.moveaxis(
        mixed_coef.reshape(4, columns, slices, 2, eigen_count), 2, 0
    )
    mixed_real = parts[:, :, :, 0]
    mixed_imag = parts[:, :, :, 1]
    left_operand = jnp.stack(
        [
            jnp.stack([mixed_real, mixed_imag], axis=2),
            jnp.stack([-mixed_imag, mixed_real], axis=2),
        ],
        axis=4,
    )
    colour_parts = [
        lax.dot_general(
            left_operand,
            eigenvectors[:, :, :, colour],
            (((4, 5), (2, 3)), ((0,), (0,))),
            preferred_element_type=jnp.float32,
        )
        for colour in range(3)
    ]
    expanded = jnp.moveaxis(jnp.stack(colour_parts, axis=3), 5, 1) * eigen_count ** (-0.5)
    return apply_twice(expanded).astype(jnp.bfloat16)


def solution(mesh):
    placed = (
        P("tm", "space", None, None, None, None, None),
        P("tm", "space", None, None, None, None, None),
        P("tm", "space", None, None, None, None, None),
        P("tm", "space", None, None, None, None),
        P("tm", None, None, None),
    )
    return jax.shard_map(
        on_device,
        mesh=mesh,
        in_specs=placed,
        out_specs=P("tm", "space", None, None, None, None, None),
        check_vma=False,
    )
```

```python
import functools

import jax
import jax.numpy as jnp
from jax import lax
from jax.experimental import pallas as pl
from jax.experimental.pallas import tpu as pltpu
from jax.sharding import PartitionSpec as P

X = 16
Y = 8

HOPPING = 0.125
HALF_MAP = (
    ((1, 0.0, -1.0), (0, 0.0, -1.0)),
    ((1, -1.0, 0.0), (0, 1.0, 0.0)),
    ((0, 0.0, -1.0), (1, 0.0, 1.0)),
    ((0, 1.0, 0.0), (1, 1.0, 0.0)),
)
ROWS = 8
LIMIT = 16 << 20
F32 = jnp.float32
BF16 = jnp.bfloat16


def dagger_map(forward_map):
    result = [None, None]
    for row_number in range(2):
        column, real_coef, imag_coef = forward_map[row_number]
        result[column] = (row_number, real_coef, -imag_coef)
    return tuple(result)


def plus(left, right, sign):
    return left + right if sign > 0 else left - right


def project(spinor, direction, sign):
    half = []
    for row, (column, a, b) in enumerate(HALF_MAP[direction]):
        real, imag = [], []
        for colour in range(3):
            if a != 0.0:
                real.append(plus(spinor(row, 0, colour), spinor(2 + column, 0, colour), sign * a))
                imag.append(plus(spinor(row, 1, colour), spinor(2 + column, 1, colour), sign * a))
            else:
                real.append(plus(spinor(row, 0, colour), spinor(2 + column, 1, colour), -sign * b))
                imag.append(plus(spinor(row, 1, colour), spinor(2 + column, 0, colour), sign * b))
        half.append([real, imag])
    return half


def link_times(link, half, adjoint):
    result = [[[None] * 3, [None] * 3] for _ in range(2)]
    for a in range(3):
        for b in range(3):
            if adjoint:
                real, imag = link(0, b, a), link(1, b, a)
            else:
                real, imag = link(0, a, b), link(1, a, b)
            for spin in range(2):
                hr, hi = half[spin][0][b], half[spin][1][b]
                if adjoint:
                    new_real = real * hr + imag * hi
                    new_imag = real * hi - imag * hr
                else:
                    new_real = real * hr - imag * hi
                    new_imag = real * hi + imag * hr
                out = result[spin]
                out[0][a] = new_real if out[0][a] is None else out[0][a] + new_real
                out[1][a] = new_imag if out[1][a] is None else out[1][a] + new_imag
    return result


def lower_terms(half, direction):
    terms = []
    for row, (column, a, b) in enumerate(dagger_map(HALF_MAP[direction])):
        for colour in range(3):
            if a != 0.0:
                terms.append((2 + row, 0, colour, a, half[column][0][colour]))
                terms.append((2 + row, 1, colour, a, half[column][1][colour]))
            else:
                terms.append((2 + row, 0, colour, -b, half[column][1][colour]))
                terms.append((2 + row, 1, colour, b, half[column][0][colour]))
    return terms


def spread(total, half, direction, lower_sign):
    for spin in range(2):
        for ri in range(2):
            for colour in range(3):
                key = (spin, ri, colour)
                total[key] = total[key] + half[spin][ri][colour]
    for spin, ri, colour, sign, value in lower_terms(half, direction):
        key = (spin, ri, colour)
        total[key] = plus(total[key], value, sign * lower_sign)


def mapped(half, function):
    return [[[function(v) for v in part] for part in spin] for spin in half]


def reader(ref, t, z, rows):
    return lambda spin, ri, colour: ref[t, z, spin, ri, colour, rows, :].astype(F32)


def link_reader(links, t, z, mu):
    return lambda ri, a, b: links[t, z, pl.ds(((mu * 3 + a) * 3 + b) * 2 + ri, 1), :]


KEYS = [(s, r, c) for s in range(4) for r in range(2) for c in range(3)]


def local_part(psi, links, clover, out):
    layers = psi.shape[1]
    slices = psi.shape[0]
    halves = psi.shape[5] // ROWS
    lane = lax.broadcasted_iota(jnp.int32, (ROWS, X * Y), 1) % X
    at_last = lane == X - 1
    at_first = lane == 0

    def ahead(direction, value):
        if direction == 1:
            return pltpu.roll(value, X * Y - X, 1)
        return jnp.where(at_last, pltpu.roll(value, X - 1, 1), pltpu.roll(value, X * Y - 1, 1))

    def behind(direction, value):
        if direction == 1:
            return pltpu.roll(value, X, 1)
        return jnp.where(at_first, pltpu.roll(value, X * Y - X + 1, 1), pltpu.roll(value, 1, 1))

    def plane(i, carry):
        t = i // (layers * halves)
        z = (i // halves) % layers
        rows = pl.ds(pl.multiple_of((i % halves) * ROWS, ROWS), ROWS)
        read = reader(psi, t, z, rows)
        total = {}
        for chiral in range(2):
            for row in range(6):
                spin, colour = 2 * chiral + row // 3, row % 3
                real = read(spin, 0, colour)
                imag = read(spin, 1, colour)
                for column in range(6):
                    at = ((chiral * 6 + row) * 6 + column) * 2
                    cr = clover[t, z, pl.ds(at, 1), :]
                    ci = clover[t, z, pl.ds(at + 1, 1), :]
                    xr = read(2 * chiral + column // 3, 0, column % 3)
                    xi = read(2 * chiral + column // 3, 1, column % 3)
                    real = real + (cr * xr - ci * xi)
                    imag = imag + (cr * xi + ci * xr)
                total[(spin, 0, colour)] = real
                total[(spin, 1, colour)] = imag
        for direction in range(2):
            link = link_reader(links, t, z, direction)
            half = mapped(project(read, direction, -1), functools.partial(ahead, direction))
            spread(total, link_times(link, half, False), direction, -1)
            half = link_times(link, project(read, direction, 1), True)
            spread(total, mapped(half, functools.partial(behind, direction)), direction, 1)
        for key in KEYS:
            out[t, z, key[0], key[1], key[2], rows, :] = total[key]
        return carry

    lax.fori_loop(0, slices * layers * halves, plane, 0)

    def bonds(direction, count, low_cell, high_cell):
        def bond(i, carry):
            other = i // halves
            rows = pl.ds(pl.multiple_of((i % halves) * ROWS, ROWS), ROWS)
            low, high = low_cell(other), high_cell(other)
            link = link_reader(links, *low, direction)
            for source, target, adjoint in ((high, low, False), (low, high, True)):
                sign = 1 if adjoint else -1
                half = link_times(link, project(reader(psi, *source, rows), direction, sign), adjoint)
                read = reader(out, *target, rows)
                total = {key: read(*key) for key in KEYS}
                spread(total, half, direction, sign)
                for key in KEYS:
                    out[target[0], target[1], key[0], key[1], key[2], rows, :] = total[key]
            return carry

        lax.fori_loop(0, count * halves, bond, 0)

    for z in range(layers - 1):
        bonds(2, slices, lambda t, z=z: (t, z), lambda t, z=z: (t, z + 1))
    for t in range(slices - 1):
        bonds(3, layers, lambda z, t=t: (t, z), lambda z, t=t: (t + 1, z))


def half_value(ref, index):
    return [
        [[ref[index, s, r, c].astype(F32) for c in range(3)] for r in range(2)] for s in range(2)
    ]


def put_half(ref, index, half):
    for s in range(2):
        for r in range(2):
            for c in range(3):
                ref[index, s, r, c] = half[s][r][c].astype(BF16)


def by_parity(place, function, pair):
    odd = place % 2 == 1
    pl.when(odd)(lambda: function(pair[0], pair[1]))
    pl.when(jnp.logical_not(odd))(lambda: function(pair[1], pair[0]))


def faces_part(psi, links, where, z_inner, z_outer, t_inner, t_outer):
    by_parity(where[0], functools.partial(z_faces, psi, links), (z_inner, z_outer))
    by_parity(where[1], functools.partial(t_faces, psi, links), (t_inner, t_outer))


def z_faces(psi, links, z_low, z_high):
    slices, layers = psi.shape[0], psi.shape[1]
    rows = slice(None)

    def of_z(t, carry):
        put_half(z_low, t, project(reader(psi, t, 0, rows), 2, -1))
        half = project(reader(psi, t, layers - 1, rows), 2, 1)
        put_half(z_high, t, link_times(link_reader(links, t, layers - 1, 2), half, True))
        return carry

    lax.fori_loop(0, slices, of_z, 0)


def t_faces(psi, links, t_low, t_high):
    slices, layers = psi.shape[0], psi.shape[1]
    rows = slice(None)

    def of_t(z, carry):
        put_half(t_low, z, project(reader(psi, 0, z, rows), 3, -1))
        half = project(reader(psi, slices - 1, z, rows), 3, 1)
        put_half(t_high, z, link_times(link_reader(links, slices - 1, z, 3), half, True))
        return carry

    lax.fori_loop(0, layers, of_t, 0)


def put(source, out, target, half, direction, sign):
    t, z = target
    read = reader(source, t, z, slice(None))
    total = {key: read(*key) for key in KEYS}
    spread(total, half, direction, sign)
    for key in KEYS:
        out[t, z, key[0], key[1], key[2]] = total[key]


def halo_part(acc, links, where, z_inner, z_outer, t_inner, t_outer, out):
    by_parity(where[0], functools.partial(z_halo, acc, links, out), (z_inner, z_outer))
    by_parity(where[1], functools.partial(t_halo, links, where, out), (t_inner, t_outer))


def z_halo(acc, links, out, z_before, z_after):
    slices, layers = acc.shape[0], acc.shape[1]

    def of_z(t, carry):
        for z in range(1, layers - 1):
            for key in KEYS:
                out[t, z, key[0], key[1], key[2]] = acc[t, z, key[0], key[1], key[2]]
        put(acc, out, (t, 0), half_value(z_before, t), 2, 1)
        half = link_times(link_reader(links, t, layers - 1, 2), half_value(z_after, t), False)
        put(acc, out, (t, layers - 1), half, 2, -1)
        return carry

    lax.fori_loop(0, slices, of_z, 0)


def t_halo(links, where, out, t_before, t_after):
    slices, layers = out.shape[0], out.shape[1]
    first = jnp.where(where[1] == 0, -1.0, 1.0).astype(F32)
    last = jnp.where(where[1] == where[2] - 1, -1.0, 1.0).astype(F32)

    def of_t(z, carry):
        put(out, out, (0, z), mapped(half_value(t_before, z), lambda v: v * first), 3, 1)
        half = mapped(half_value(t_after, z), lambda v: v * last)
        half = link_times(link_reader(links, slices - 1, z, 3), half, False)
        put(out, out, (slices - 1, z), half, 3, -1)
        return carry

    lax.fori_loop(0, layers, of_t, 0)


def position():
    return lax.axis_index("space"), lax.axis_index("tm"), lax.axis_size("tm")


VMEM = pl.BlockSpec(memory_space=pltpu.VMEM)
SMEM = pl.BlockSpec(memory_space=pltpu.SMEM)


def call(kernel, in_count, out_shapes, scratch=(), smem=(), flops=1 << 22, name=None):
    specs = [SMEM if i in smem else VMEM for i in range(in_count)]
    return pl.pallas_call(
        kernel,
        out_shape=out_shapes,
        in_specs=specs,
        out_specs=jax.tree.map(lambda _: VMEM, out_shapes),
        scratch_shapes=list(scratch),
        cost_estimate=pl.CostEstimate(flops=flops, bytes_accessed=1 << 21, transcendentals=0),
        compiler_params=pltpu.CompilerParams(vmem_limit_bytes=LIMIT),
        name=name,
    )


def entry_kernel(source, gauge, psi, links, *sent):
    psi[...] = source[...].astype(F32)
    slices, layers = source.shape[0], source.shape[1]
    for t in range(slices):
        for z in range(layers):
            for mu in range(4):
                for a in range(3):
                    for b in range(3):
                        row = ((mu * 3 + a) * 3 + b) * 2
                        value = gauge[t, z, mu, a, b].astype(F32)
                        links[t, z, pl.ds(row, 2), :] = value * (-HOPPING)
    faces_part(psi, links, position(), *sent)


def clover_kernel(clover, rows):
    slices, layers = clover.shape[0], clover.shape[1]
    for t in range(slices):
        for z in range(layers):
            for chiral in range(2):
                for i in range(6):
                    for j in range(6):
                        row = ((chiral * 6 + i) * 6 + j) * 2
                        rows[t, z, pl.ds(row, 2), :] = clover[t, z, chiral, i, j].astype(F32)


def local_kernel(psi, links, clover, out):
    local_part(psi, links, clover, out)


def middle_kernel(acc, links, *refs):
    received, (psi, *sent) = refs[:4], refs[4:]
    halo_part(acc, links, position(), *received, psi)
    faces_part(psi, links, position(), *sent)


def last_kernel(acc, links, *refs):
    received, (result, psi) = refs[:4], refs[4:]
    halo_part(acc, links, position(), *received, psi)
    result[...] = psi[...].astype(BF16)


def coefficient_kernel(scale, acc, links, *refs):
    received, (vectors, result, psi, rounded) = refs[:4], refs[4:]
    halo_part(acc, links, position(), *received, psi)
    slices, layers = acc.shape[0], acc.shape[1]
    columns = acc.shape[5]
    half_count = vectors.shape[4] // 128
    for t in range(slices):
        for z in range(layers):
            for colour in range(3):
                for spin in range(4):
                    for ri in range(2):
                        row = (ri * 4 + spin) * columns
                        rounded[t, z, colour, pl.ds(row, columns), :] = psi[
                            t, z, spin, ri, colour
                        ].astype(BF16)
    side = 4 * columns
    for t in range(slices):
        sums = []
        for part in range(2):
            total = None
            for z in range(layers):
                for colour in range(3):
                    product = lax.dot_general(
                        rounded[t, z, colour],
                        vectors[t, z, part, colour],
                        (((1,), (1,)), ((), ())),
                        preferred_element_type=F32,
                    )
                    total = product if total is None else total + product
            sums.append(total)
        real = (sums[0][:side] + sums[1][side:]) * scale
        imag = (sums[0][side:] - sums[1][:side]) * scale
        for ri, value in enumerate((real, imag)):
            for k in range(half_count):
                row = (t * 2 + ri) * half_count + k
                result[:, row, :] = value[:, k * 128 : (k + 1) * 128]


def mix_kernel(shares, elemental, result):
    slices = elemental.shape[0]
    eigen_count = elemental.shape[2]
    half_count = eigen_count // 128
    total = jnp.sum(shares[...], axis=0)

    def pieces(value):
        first = value.astype(BF16)
        rest = value - first.astype(F32)
        second = rest.astype(BF16)
        third = (rest - second.astype(F32)).astype(BF16)
        return [first, second, third]

    def row_of(t, ri):
        start = (t * 2 + ri) * half_count
        return jnp.concatenate([total[start + k : start + k + 1] for k in range(half_count)], axis=1)

    for t in range(slices):
        parts = jnp.concatenate([row_of(t, 0), row_of(t, 1)], axis=0)
        terms = []
        for component in range(2):
            weights = elemental[t, component]
            whole = None
            for piece in pieces(parts):
                product = lax.dot_general(
                    piece, weights, (((1,), (1,)), ((), ())), preferred_element_type=F32
                )
                whole = product if whole is None else whole + product
            terms.append(whole)
        real = terms[0][0:1] - terms[1][1:2]
        imag = terms[0][1:2] + terms[1][0:1]
        for ri, value in enumerate((real, imag)):
            for k in range(half_count):
                row = (t * 2 + ri) * half_count + k
                piece = value[:, k * 128 : (k + 1) * 128].astype(BF16)
                result[:, row : row + 1, :] = jnp.broadcast_to(
                    piece[None], (result.shape[0], 1, 128)
                )


def expand_kernel(mixed, vectors, links, psi, *refs):
    sent, (turned, left) = refs[:4], refs[4:]
    slices, layers = psi.shape[0], psi.shape[1]
    columns = psi.shape[5]
    eigen_count = vectors.shape[4]
    half_count = eigen_count // 128
    side = 4 * columns
    scale = eigen_count ** (-0.5)
    turned[...] = mixed[...].astype(F32)
    for t in range(slices):
        for ri in range(2):
            for k in range(half_count):
                row = (t * 2 + ri) * half_count + k
                value = turned[:, row, :]
                lanes = slice(k * 128, (k + 1) * 128)
                own = value.astype(BF16)
                if ri == 0:
                    left[0, :side, lanes] = own
                    left[1, side:, lanes] = own
                else:
                    left[0, side:, lanes] = own
                    left[1, :side, lanes] = (-value).astype(BF16)
        for z in range(layers):
            for colour in range(3):
                value = jnp.dot(left[0], vectors[t, z, 0, colour], preferred_element_type=F32)
                value += jnp.dot(left[1], vectors[t, z, 1, colour], preferred_element_type=F32)
                value = value * scale
                for ri in range(2):
                    for spin in range(4):
                        row = (ri * 4 + spin) * columns
                        psi[t, z, spin, ri, colour] = value[row : row + columns]
    faces_part(psi, links, position(), *sent)


def on_device(source, gauge_links, clover, eigenvectors, elemental):
    slices, layers = source.shape[0], source.shape[1]
    columns, sites = source.shape[5], source.shape[6]
    eigen_count = eigenvectors.shape[4]
    space_count = lax.axis_size("space")
    spinor_type = jax.ShapeDtypeStruct(source.shape, F32)
    z_face = jax.ShapeDtypeStruct((slices, 2, 2, 3, columns, sites), BF16)
    t_face = jax.ShapeDtypeStruct((layers, 2, 2, 3, columns, sites), BF16)
    faces = (z_face, z_face, t_face, t_face)
    link_rows = jax.ShapeDtypeStruct((slices, layers, 72, sites), F32)
    clover_rows = jax.ShapeDtypeStruct((slices, layers, 144, sites), F32)
    row_count = slices * 2 * eigen_count // 128

    def swapped(value, axis, offset):
        count = lax.axis_size(axis)
        pairs = [(i % count, (i + 1) % count) for i in range(offset, count + offset, 2)]
        return lax.ppermute(value, axis, pairs + [(b, a) for a, b in pairs])

    def exchanged(z_inner, z_outer, t_inner, t_outer):
        z_far = swapped(z_outer, "space", 1)
        t_far = swapped(t_outer, "tm", 1)
        return swapped(z_inner, "space", 0), z_far, swapped(t_inner, "tm", 0), t_far

    psi, links, *sent = call(
        entry_kernel, 2, (spinor_type, link_rows) + faces, name="entry"
    )(source, jnp.transpose(gauge_links, (0, 1, 2, 4, 5, 3, 6)))
    got = exchanged(*sent)
    clover_f32 = call(clover_kernel, 1, clover_rows, name="clover_rows")(
        jnp.transpose(clover, (0, 1, 2, 4, 5, 3, 6))
    )

    def local(spinor):
        return call(local_kernel, 3, spinor_type, flops=1 << 26, name="local")(
            spinor, links, clover_f32
        )

    def middle(acc, received):
        return call(middle_kernel, 6, (spinor_type,) + faces, name="middle")(
            acc, links, *received
        )

    acc = local(psi)
    psi, *sent = middle(acc, got)
    got = exchanged(*sent)
    acc = local(psi)
    normaliser = (3.0 * X * Y * layers * space_count) ** (-0.5)
    scratch_psi = pltpu.VMEM(source.shape, F32)
    partial_sums = call(
        functools.partial(coefficient_kernel, normaliser),
        7,
        jax.ShapeDtypeStruct((4 * columns, row_count, 128), F32),
        scratch=(scratch_psi, pltpu.VMEM((slices, layers, 3, 8 * columns, sites), BF16)),
        name="coefficients",
    )(acc, links, *got, eigenvectors)
    shares = lax.all_to_all(partial_sums, "space", 0, 0, tiled=True)
    mixed = call(
        mix_kernel,
        2,
        jax.ShapeDtypeStruct((space_count, row_count, 128), BF16),
        name="mix",
    )(shares, elemental)
    mixed = lax.all_to_all(mixed, "space", 0, 0, tiled=True)
    psi, *sent = call(
        expand_kernel,
        3,
        (spinor_type,) + faces,
        scratch=(
            pltpu.VMEM((4 * columns, row_count, 128), F32),
            pltpu.VMEM((2, 8 * columns, eigen_count), BF16),
        ),
        name="expand",
    )(mixed, eigenvectors, links)
    got = exchanged(*sent)
    acc = local(psi)
    psi, *sent = middle(acc, got)
    got = exchanged(*sent)
    acc = local(psi)
    return call(
        last_kernel,
        6,
        jax.ShapeDtypeStruct(source.shape, BF16),
        scratch=(scratch_psi,),
        name="last",
    )(acc, links, *got)


def solution(mesh):
    placed = (
        P("tm", "space", None, None, None, None, None),
        P("tm", "space", None, None, None, None, None),
        P("tm", "space", None, None, None, None, None),
        P("tm", "space", None, None, None, None),
        P("tm", None, None, None),
    )
    return jax.shard_map(
        on_device,
        mesh=mesh,
        in_specs=placed,
        out_specs=P("tm", "space", None, None, None, None, None),
        check_vma=False,
    )
```

```python
import functools

import jax
import jax.numpy as jnp
from jax import lax
from jax.experimental import pallas as pl
from jax.experimental.pallas import tpu as pltpu
from jax.sharding import PartitionSpec as P

X = 16
Y = 8

HOPPING = 0.125
HALF_MAP = (
    ((1, 0.0, -1.0), (0, 0.0, -1.0)),
    ((1, -1.0, 0.0), (0, 1.0, 0.0)),
    ((0, 0.0, -1.0), (1, 0.0, 1.0)),
    ((0, 1.0, 0.0), (1, 1.0, 0.0)),
)
ROWS = 8
LIMIT = 16 << 20
F32 = jnp.float32
BF16 = jnp.bfloat16


def dagger_map(forward_map):
    result = [None, None]
    for row_number in range(2):
        column, real_coef, imag_coef = forward_map[row_number]
        result[column] = (row_number, real_coef, -imag_coef)
    return tuple(result)


def plus(left, right, sign):
    return left + right if sign > 0 else left - right


def project(spinor, direction, sign):
    half = []
    for row, (column, a, b) in enumerate(HALF_MAP[direction]):
        real, imag = [], []
        for colour in range(3):
            if a != 0.0:
                real.append(plus(spinor(row, 0, colour), spinor(2 + column, 0, colour), sign * a))
                imag.append(plus(spinor(row, 1, colour), spinor(2 + column, 1, colour), sign * a))
            else:
                real.append(plus(spinor(row, 0, colour), spinor(2 + column, 1, colour), -sign * b))
                imag.append(plus(spinor(row, 1, colour), spinor(2 + column, 0, colour), sign * b))
        half.append([real, imag])
    return half


def products(rows, vector, sums, conjugate):
    real, less, more = rows
    vr, vi, both = vector
    terms = (real * both, more * vr, less * vi) if conjugate else (real * both, less * vr, more * vi)
    return list(terms) if sums is None else [old + new for old, new in zip(sums, terms)]


def total_of(sums, conjugate):
    if conjugate:
        return sums[0] + sums[2], sums[0] - sums[1]
    return sums[0] - sums[2], sums[0] + sums[1]


def link_times(link, half, adjoint):
    result = [[[None] * 3, [None] * 3] for _ in range(2)]
    vectors = [
        [(h[0][b], h[1][b], h[0][b] + h[1][b]) for b in range(3)] for h in half
    ]
    for a in range(3):
        sums = [None, None]
        for b in range(3):
            rows = link(b, a) if adjoint else link(a, b)
            for spin in range(2):
                sums[spin] = products(rows, vectors[spin][b], sums[spin], adjoint)
        for spin in range(2):
            result[spin][0][a], result[spin][1][a] = total_of(sums[spin], adjoint)
    return result


def lower_terms(half, direction):
    terms = []
    for row, (column, a, b) in enumerate(dagger_map(HALF_MAP[direction])):
        for colour in range(3):
            if a != 0.0:
                terms.append((2 + row, 0, colour, a, half[column][0][colour]))
                terms.append((2 + row, 1, colour, a, half[column][1][colour]))
            else:
                terms.append((2 + row, 0, colour, -b, half[column][1][colour]))
                terms.append((2 + row, 1, colour, b, half[column][0][colour]))
    return terms


def spread(total, half, direction, lower_sign):
    for spin in range(2):
        for ri in range(2):
            for colour in range(3):
                key = (spin, ri, colour)
                total[key] = total[key] + half[spin][ri][colour]
    for spin, ri, colour, sign, value in lower_terms(half, direction):
        key = (spin, ri, colour)
        total[key] = plus(total[key], value, sign * lower_sign)


def mapped(half, function):
    return [[[function(v) for v in part] for part in spin] for spin in half]


def reader(ref, t, z, rows):
    return lambda spin, ri, colour: ref[t, z, spin, ri, colour, rows, :].astype(F32)


def three_rows(ref, t, z, entry):
    return [ref[t, z, pl.ds(entry * 3 + i, 1), :] for i in range(3)]


def put_three_rows(ref, t, z, entry, value):
    real, imag = value[0:1], value[1:2]
    for i, row in enumerate((real, imag - real, imag + real)):
        ref[t, z, pl.ds(entry * 3 + i, 1), :] = row


def link_reader(links, t, z, mu):
    return lambda a, b: three_rows(links, t, z, (mu * 3 + a) * 3 + b)


KEYS = [(s, r, c) for s in range(4) for r in range(2) for c in range(3)]


def local_part(psi, links, clover, out):
    layers = psi.shape[1]
    slices = psi.shape[0]
    halves = psi.shape[5] // ROWS
    lane = lax.broadcasted_iota(jnp.int32, (ROWS, X * Y), 1) % X
    at_last = lane == X - 1
    at_first = lane == 0

    def ahead(direction, value):
        if direction == 1:
            return pltpu.roll(value, X * Y - X, 1)
        return jnp.where(at_last, pltpu.roll(value, X - 1, 1), pltpu.roll(value, X * Y - 1, 1))

    def behind(direction, value):
        if direction == 1:
            return pltpu.roll(value, X, 1)
        return jnp.where(at_first, pltpu.roll(value, X * Y - X + 1, 1), pltpu.roll(value, 1, 1))

    def plane(i, carry):
        t = i // (layers * halves)
        z = (i // halves) % layers
        rows = pl.ds(pl.multiple_of((i % halves) * ROWS, ROWS), ROWS)
        read = reader(psi, t, z, rows)
        total = {}
        for chiral in range(2):
            vectors = []
            for column in range(6):
                real = read(2 * chiral + column // 3, 0, column % 3)
                imag = read(2 * chiral + column // 3, 1, column % 3)
                vectors.append((real, imag, real + imag))
            for row in range(6):
                spin, colour = 2 * chiral + row // 3, row % 3
                sums = None
                for column in range(6):
                    entry = three_rows(clover, t, z, (chiral * 6 + row) * 6 + column)
                    sums = products(entry, vectors[column], sums, False)
                real, imag = total_of(sums, False)
                total[(spin, 0, colour)] = vectors[row][0] + real
                total[(spin, 1, colour)] = vectors[row][1] + imag
        for direction in range(2):
            link = link_reader(links, t, z, direction)
            half = mapped(project(read, direction, -1), functools.partial(ahead, direction))
            spread(total, link_times(link, half, False), direction, -1)
            half = link_times(link, project(read, direction, 1), True)
            spread(total, mapped(half, functools.partial(behind, direction)), direction, 1)
        for key in KEYS:
            out[t, z, key[0], key[1], key[2], rows, :] = total[key]
        return carry

    lax.fori_loop(0, slices * layers * halves, plane, 0)

    def bonds(direction, count, low_cell, high_cell):
        def bond(i, carry):
            other = i // halves
            rows = pl.ds(pl.multiple_of((i % halves) * ROWS, ROWS), ROWS)
            low, high = low_cell(other), high_cell(other)
            link = link_reader(links, *low, direction)
            for source, target, adjoint in ((high, low, False), (low, high, True)):
                sign = 1 if adjoint else -1
                half = link_times(link, project(reader(psi, *source, rows), direction, sign), adjoint)
                read = reader(out, *target, rows)
                total = {key: read(*key) for key in KEYS}
                spread(total, half, direction, sign)
                for key in KEYS:
                    out[target[0], target[1], key[0], key[1], key[2], rows, :] = total[key]
            return carry

        lax.fori_loop(0, count * halves, bond, 0)

    for z in range(layers - 1):
        bonds(2, slices, lambda t, z=z: (t, z), lambda t, z=z: (t, z + 1))
    for t in range(slices - 1):
        bonds(3, layers, lambda z, t=t: (t, z), lambda z, t=t: (t + 1, z))


def half_value(ref, index):
    return [
        [[ref[index, s, r, c].astype(F32) for c in range(3)] for r in range(2)] for s in range(2)
    ]


def put_half(ref, index, half):
    for s in range(2):
        for r in range(2):
            for c in range(3):
                ref[index, s, r, c] = half[s][r][c].astype(BF16)


def by_parity(place, function, pair):
    odd = place % 2 == 1
    pl.when(odd)(lambda: function(pair[0], pair[1]))
    pl.when(jnp.logical_not(odd))(lambda: function(pair[1], pair[0]))


def faces_part(psi, links, where, z_outer, z_inner, t_outer, t_inner):
    by_parity(where[0], functools.partial(z_faces, psi, links), (z_inner, z_outer))
    by_parity(where[1], functools.partial(t_faces, psi, links), (t_inner, t_outer))


def z_faces(psi, links, z_low, z_high):
    slices, layers = psi.shape[0], psi.shape[1]
    rows = slice(None)

    def of_z(t, carry):
        put_half(z_low, t, project(reader(psi, t, 0, rows), 2, -1))
        half = project(reader(psi, t, layers - 1, rows), 2, 1)
        put_half(z_high, t, link_times(link_reader(links, t, layers - 1, 2), half, True))
        return carry

    lax.fori_loop(0, slices, of_z, 0)


def t_faces(psi, links, t_low, t_high):
    slices, layers = psi.shape[0], psi.shape[1]
    rows = slice(None)

    def of_t(z, carry):
        put_half(t_low, z, project(reader(psi, 0, z, rows), 3, -1))
        half = project(reader(psi, slices - 1, z, rows), 3, 1)
        put_half(t_high, z, link_times(link_reader(links, slices - 1, z, 3), half, True))
        return carry

    lax.fori_loop(0, layers, of_t, 0)


def put(source, out, target, half, direction, sign):
    t, z = target
    read = reader(source, t, z, slice(None))
    total = {key: read(*key) for key in KEYS}
    spread(total, half, direction, sign)
    for key in KEYS:
        out[t, z, key[0], key[1], key[2]] = total[key]


def halo_part(acc, links, where, z_outer, z_inner, t_outer, t_inner, out):
    by_parity(where[0], functools.partial(z_halo, acc, links, out), (z_inner, z_outer))
    by_parity(where[1], functools.partial(t_halo, links, where, out), (t_inner, t_outer))


def z_halo(acc, links, out, z_before, z_after):
    slices, layers = acc.shape[0], acc.shape[1]

    def of_z(t, carry):
        for z in range(1, layers - 1):
            for key in KEYS:
                out[t, z, key[0], key[1], key[2]] = acc[t, z, key[0], key[1], key[2]]
        put(acc, out, (t, 0), half_value(z_before, t), 2, 1)
        half = link_times(link_reader(links, t, layers - 1, 2), half_value(z_after, t), False)
        put(acc, out, (t, layers - 1), half, 2, -1)
        return carry

    lax.fori_loop(0, slices, of_z, 0)


def t_halo(links, where, out, t_before, t_after):
    slices, layers = out.shape[0], out.shape[1]
    first = jnp.where(where[1] == 0, -1.0, 1.0).astype(F32)
    last = jnp.where(where[1] == where[2] - 1, -1.0, 1.0).astype(F32)

    def of_t(z, carry):
        put(out, out, (0, z), mapped(half_value(t_before, z), lambda v: v * first), 3, 1)
        half = mapped(half_value(t_after, z), lambda v: v * last)
        half = link_times(link_reader(links, slices - 1, z, 3), half, False)
        put(out, out, (slices - 1, z), half, 3, -1)
        return carry

    lax.fori_loop(0, layers, of_t, 0)


def position():
    return lax.axis_index("space"), lax.axis_index("tm"), lax.axis_size("tm")


VMEM = pl.BlockSpec(memory_space=pltpu.VMEM)
FAR = pl.BlockSpec(memory_space=pltpu.HBM)


def in_far(value):
    return pltpu.with_memory_space_constraint(value, pltpu.HBM)


def call(kernel, in_count, out_shapes, scratch=(), far=(), flops=1 << 22, name=None):
    specs = [FAR if i in far else VMEM for i in range(in_count)]
    return pl.pallas_call(
        kernel,
        out_shape=out_shapes,
        in_specs=specs,
        out_specs=jax.tree.map(lambda _: VMEM, out_shapes),
        scratch_shapes=list(scratch),
        cost_estimate=pl.CostEstimate(flops=flops, bytes_accessed=1 << 21, transcendentals=0),
        compiler_params=pltpu.CompilerParams(vmem_limit_bytes=LIMIT),
        name=name,
    )


def entry_kernel(source_far, gauge_far, psi, links, *refs):
    sent, (source, gauge, arrived) = refs[:4], refs[4:]
    gauge_copy = pltpu.make_async_copy(gauge_far, gauge, arrived.at[0])
    source_copy = pltpu.make_async_copy(source_far, source, arrived.at[1])
    gauge_copy.start()
    source_copy.start()
    gauge_copy.wait()
    slices, layers = source.shape[0], source.shape[1]
    for t in range(slices):
        for z in range(layers):
            for mu in range(4):
                for a in range(3):
                    for b in range(3):
                        value = gauge[t, z, mu, a, b].astype(F32) * (-HOPPING)
                        put_three_rows(links, t, z, (mu * 3 + a) * 3 + b, value)
    source_copy.wait()
    psi[...] = source[...].astype(F32)
    faces_part(psi, links, position(), *sent)


def clover_kernel(clover, rows):
    slices, layers = clover.shape[0], clover.shape[1]
    for t in range(slices):
        for z in range(layers):
            for chiral in range(2):
                for i in range(6):
                    for j in range(6):
                        value = clover[t, z, chiral, i, j].astype(F32)
                        put_three_rows(rows, t, z, (chiral * 6 + i) * 6 + j, value)


def local_kernel(psi, links, clover, out):
    local_part(psi, links, clover, out)


def middle_kernel(acc, links, *refs):
    received, (psi, *sent) = refs[:4], refs[4:]
    halo_part(acc, links, position(), *received, psi)
    faces_part(psi, links, position(), *sent)


def last_kernel(acc, links, *refs):
    received, (result, psi) = refs[:4], refs[4:]
    halo_part(acc, links, position(), *received, psi)
    result[...] = psi[...].astype(BF16)


def coefficient_kernel(scale, acc, links, *refs):
    received, (vectors, result, psi, rounded) = refs[:4], refs[4:]
    halo_part(acc, links, position(), *received, psi)
    slices, layers = acc.shape[0], acc.shape[1]
    columns = acc.shape[5]
    half_count = vectors.shape[4] // 128
    for t in range(slices):
        for z in range(layers):
            for colour in range(3):
                for spin in range(4):
                    for ri in range(2):
                        row = (ri * 4 + spin) * columns
                        rounded[t, z, colour, pl.ds(row, columns), :] = psi[
                            t, z, spin, ri, colour
                        ].astype(BF16)
    side = 4 * columns
    for t in range(slices):
        sums = []
        for part in range(2):
            total = None
            for z in range(layers):
                for colour in range(3):
                    product = lax.dot_general(
                        rounded[t, z, colour],
                        vectors[t, z, part, colour],
                        (((1,), (1,)), ((), ())),
                        preferred_element_type=F32,
                    )
                    total = product if total is None else total + product
            sums.append(total)
        real = (sums[0][:side] + sums[1][side:]) * scale
        imag = (sums[0][side:] - sums[1][:side]) * scale
        for ri, value in enumerate((real, imag)):
            for k in range(half_count):
                row = (t * 2 + ri) * half_count + k
                result[:, row, :] = value[:, k * 128 : (k + 1) * 128]


def mix_kernel(shares, elemental, result):
    slices = elemental.shape[0]
    eigen_count = elemental.shape[2]
    half_count = eigen_count // 128
    total = jnp.sum(shares[...], axis=0)

    def pieces(value):
        first = value.astype(BF16)
        rest = value - first.astype(F32)
        second = rest.astype(BF16)
        third = (rest - second.astype(F32)).astype(BF16)
        return [first, second, third]

    def row_of(t, ri):
        start = (t * 2 + ri) * half_count
        return jnp.concatenate([total[start + k : start + k + 1] for k in range(half_count)], axis=1)

    for t in range(slices):
        parts = jnp.concatenate([row_of(t, 0), row_of(t, 1)], axis=0)
        terms = []
        for component in range(2):
            weights = elemental[t, component]
            whole = None
            for piece in pieces(parts):
                product = lax.dot_general(
                    piece, weights, (((1,), (1,)), ((), ())), preferred_element_type=F32
                )
                whole = product if whole is None else whole + product
            terms.append(whole)
        real = terms[0][0:1] - terms[1][1:2]
        imag = terms[0][1:2] + terms[1][0:1]
        for ri, value in enumerate((real, imag)):
            for k in range(half_count):
                row = (t * 2 + ri) * half_count + k
                piece = value[:, k * 128 : (k + 1) * 128].astype(BF16)
                result[:, row : row + 1, :] = jnp.broadcast_to(
                    piece[None], (result.shape[0], 1, 128)
                )


def expand_kernel(mixed, vectors, links, psi, *refs):
    sent, (turned, left) = refs[:4], refs[4:]
    slices, layers = psi.shape[0], psi.shape[1]
    columns = psi.shape[5]
    eigen_count = vectors.shape[4]
    half_count = eigen_count // 128
    side = 4 * columns
    scale = eigen_count ** (-0.5)
    turned[...] = mixed[...].astype(F32)
    for t in range(slices):
        for ri in range(2):
            for k in range(half_count):
                row = (t * 2 + ri) * half_count + k
                value = turned[:, row, :]
                lanes = slice(k * 128, (k + 1) * 128)
                own = value.astype(BF16)
                if ri == 0:
                    left[0, :side, lanes] = own
                    left[1, side:, lanes] = own
                else:
                    left[0, side:, lanes] = own
                    left[1, :side, lanes] = (-value).astype(BF16)
        for z in range(layers):
            for colour in range(3):
                value = jnp.dot(left[0], vectors[t, z, 0, colour], preferred_element_type=F32)
                value += jnp.dot(left[1], vectors[t, z, 1, colour], preferred_element_type=F32)
                value = value * scale
                for ri in range(2):
                    for spin in range(4):
                        row = (ri * 4 + spin) * columns
                        psi[t, z, spin, ri, colour] = value[row : row + columns]
    faces_part(psi, links, position(), *sent)


def on_device(source, gauge_links, clover, eigenvectors, elemental):
    slices, layers = source.shape[0], source.shape[1]
    columns, sites = source.shape[5], source.shape[6]
    eigen_count = eigenvectors.shape[4]
    space_count = lax.axis_size("space")
    spinor_type = jax.ShapeDtypeStruct(source.shape, F32)
    z_face = jax.ShapeDtypeStruct((slices, 2, 2, 3, columns, sites), BF16)
    t_face = jax.ShapeDtypeStruct((layers, 2, 2, 3, columns, sites), BF16)
    faces = (z_face, z_face, t_face, t_face)
    link_rows = jax.ShapeDtypeStruct((slices, layers, 108, sites), F32)
    clover_rows = jax.ShapeDtypeStruct((slices, layers, 216, sites), F32)
    row_count = slices * 2 * eigen_count // 128

    def swapped(value, axis, offset):
        count = lax.axis_size(axis)
        pairs = [(i % count, (i + 1) % count) for i in range(offset, count + offset, 2)]
        return lax.ppermute(value, axis, pairs + [(b, a) for a, b in pairs])

    def exchanged(z_outer, z_inner, t_outer, t_inner):
        return (
            swapped(z_outer, "space", 1),
            swapped(z_inner, "space", 0),
            swapped(t_outer, "tm", 1),
            swapped(t_inner, "tm", 0),
        )

    gauge = jnp.transpose(gauge_links, (0, 1, 2, 4, 5, 3, 6))
    psi, links, *sent = call(
        entry_kernel,
        2,
        (spinor_type, link_rows) + faces,
        scratch=(
            pltpu.VMEM(source.shape, BF16),
            pltpu.VMEM(gauge.shape, BF16),
            pltpu.SemaphoreType.DMA((2,)),
        ),
        far=(0, 1),
        name="entry",
    )(in_far(source), in_far(gauge))
    got = exchanged(*sent)
    clover_f32 = call(clover_kernel, 1, clover_rows, name="clover_rows")(
        jnp.transpose(clover, (0, 1, 2, 4, 5, 3, 6))
    )

    def local(spinor):
        return call(local_kernel, 3, spinor_type, flops=1 << 26, name="local")(
            spinor, links, clover_f32
        )

    def middle(acc, received):
        return call(middle_kernel, 6, (spinor_type,) + faces, name="middle")(
            acc, links, *received
        )

    acc = local(psi)
    psi, *sent = middle(acc, got)
    got = exchanged(*sent)
    acc = local(psi)
    normaliser = (3.0 * X * Y * layers * space_count) ** (-0.5)
    scratch_psi = pltpu.VMEM(source.shape, F32)
    partial_sums = call(
        functools.partial(coefficient_kernel, normaliser),
        7,
        jax.ShapeDtypeStruct((4 * columns, row_count, 128), F32),
        scratch=(scratch_psi, pltpu.VMEM((slices, layers, 3, 8 * columns, sites), BF16)),
        name="coefficients",
    )(acc, links, *got, eigenvectors)
    shares = lax.all_to_all(partial_sums, "space", 0, 0, tiled=True)
    mixed = call(
        mix_kernel,
        2,
        jax.ShapeDtypeStruct((space_count, row_count, 128), BF16),
        name="mix",
    )(shares, elemental)
    mixed = lax.all_to_all(mixed, "space", 0, 0, tiled=True)
    psi, *sent = call(
        expand_kernel,
        3,
        (spinor_type,) + faces,
        scratch=(
            pltpu.VMEM((4 * columns, row_count, 128), F32),
            pltpu.VMEM((2, 8 * columns, eigen_count), BF16),
        ),
        name="expand",
    )(mixed, eigenvectors, links)
    got = exchanged(*sent)
    acc = local(psi)
    psi, *sent = middle(acc, got)
    got = exchanged(*sent)
    acc = local(psi)
    return call(
        last_kernel,
        6,
        jax.ShapeDtypeStruct(source.shape, BF16),
        scratch=(scratch_psi,),
        name="last",
    )(acc, links, *got)


def solution(mesh):
    placed = (
        P("tm", "space", None, None, None, None, None),
        P("tm", "space", None, None, None, None, None),
        P("tm", "space", None, None, None, None, None),
        P("tm", "space", None, None, None, None),
        P("tm", None, None, None),
    )
    return jax.shard_map(
        on_device,
        mesh=mesh,
        in_specs=placed,
        out_specs=P("tm", "space", None, None, None, None, None),
        check_vma=False,
    )
```

```python
import functools

import jax
import jax.numpy as jnp
from jax import lax
from jax.experimental import pallas as pl
from jax.experimental.pallas import tpu as pltpu
from jax.sharding import PartitionSpec as P

X = 16
Y = 8

HOPPING = 0.125
HALF_MAP = (
    ((1, 0.0, -1.0), (0, 0.0, -1.0)),
    ((1, -1.0, 0.0), (0, 1.0, 0.0)),
    ((0, 0.0, -1.0), (1, 0.0, 1.0)),
    ((0, 1.0, 0.0), (1, 1.0, 0.0)),
)
ROWS = 8
LIMIT = 16 << 20
F32 = jnp.float32
BF16 = jnp.bfloat16


def dagger_map(forward_map):
    result = [None, None]
    for row_number in range(2):
        column, real_coef, imag_coef = forward_map[row_number]
        result[column] = (row_number, real_coef, -imag_coef)
    return tuple(result)


def plus(left, right, sign):
    return left + right if sign > 0 else left - right


def project(spinor, direction, sign):
    half = []
    for row, (column, a, b) in enumerate(HALF_MAP[direction]):
        real, imag = [], []
        for colour in range(3):
            if a != 0.0:
                real.append(plus(spinor(row, 0, colour), spinor(2 + column, 0, colour), sign * a))
                imag.append(plus(spinor(row, 1, colour), spinor(2 + column, 1, colour), sign * a))
            else:
                real.append(plus(spinor(row, 0, colour), spinor(2 + column, 1, colour), -sign * b))
                imag.append(plus(spinor(row, 1, colour), spinor(2 + column, 0, colour), sign * b))
        half.append([real, imag])
    return half


def products(rows, vector, sums, conjugate):
    real, less, more = rows
    vr, vi, both = vector
    terms = (real * both, more * vr, less * vi) if conjugate else (real * both, less * vr, more * vi)
    return list(terms) if sums is None else [old + new for old, new in zip(sums, terms)]


def total_of(sums, conjugate):
    if conjugate:
        return sums[0] + sums[2], sums[0] - sums[1]
    return sums[0] - sums[2], sums[0] + sums[1]


def link_times(link, half, adjoint):
    result = [[[None] * 3, [None] * 3] for _ in range(2)]
    vectors = [
        [(h[0][b], h[1][b], h[0][b] + h[1][b]) for b in range(3)] for h in half
    ]
    for a in range(3):
        sums = [None, None]
        for b in range(3):
            rows = link(b, a) if adjoint else link(a, b)
            for spin in range(2):
                sums[spin] = products(rows, vectors[spin][b], sums[spin], adjoint)
        for spin in range(2):
            result[spin][0][a], result[spin][1][a] = total_of(sums[spin], adjoint)
    return result


def lower_terms(half, direction):
    terms = []
    for row, (column, a, b) in enumerate(dagger_map(HALF_MAP[direction])):
        for colour in range(3):
            if a != 0.0:
                terms.append((2 + row, 0, colour, a, half[column][0][colour]))
                terms.append((2 + row, 1, colour, a, half[column][1][colour]))
            else:
                terms.append((2 + row, 0, colour, -b, half[column][1][colour]))
                terms.append((2 + row, 1, colour, b, half[column][0][colour]))
    return terms


def spread(total, half, direction, lower_sign):
    for spin in range(2):
        for ri in range(2):
            for colour in range(3):
                key = (spin, ri, colour)
                total[key] = total[key] + half[spin][ri][colour]
    for spin, ri, colour, sign, value in lower_terms(half, direction):
        key = (spin, ri, colour)
        total[key] = plus(total[key], value, sign * lower_sign)


def mapped(half, function):
    return [[[function(v) for v in part] for part in spin] for spin in half]


def reader(ref, t, z, rows):
    return lambda spin, ri, colour: ref[t, z, spin, ri, colour, rows, :].astype(F32)


def three_rows(ref, t, z, entry):
    return [ref[t, z, pl.ds(entry * 3 + i, 1), :] for i in range(3)]


def put_three_rows(ref, t, z, entry, value):
    real, imag = value[0:1], value[1:2]
    for i, row in enumerate((real, imag - real, imag + real)):
        ref[t, z, pl.ds(entry * 3 + i, 1), :] = row


def link_reader(links, t, z, mu):
    return lambda a, b: three_rows(links, t, z, (mu * 3 + a) * 3 + b)


KEYS = [(s, r, c) for s in range(4) for r in range(2) for c in range(3)]


def local_part(psi, links, clover, out):
    layers = psi.shape[1]
    slices = psi.shape[0]
    halves = psi.shape[5] // ROWS
    lane = lax.broadcasted_iota(jnp.int32, (ROWS, X * Y), 1) % X
    at_last = lane == X - 1
    at_first = lane == 0

    def ahead(direction, value):
        if direction == 1:
            return pltpu.roll(value, X * Y - X, 1)
        return jnp.where(at_last, pltpu.roll(value, X - 1, 1), pltpu.roll(value, X * Y - 1, 1))

    def behind(direction, value):
        if direction == 1:
            return pltpu.roll(value, X, 1)
        return jnp.where(at_first, pltpu.roll(value, X * Y - X + 1, 1), pltpu.roll(value, 1, 1))

    def plane(i, carry):
        t = i // (layers * halves)
        z = (i // halves) % layers
        rows = pl.ds(pl.multiple_of((i % halves) * ROWS, ROWS), ROWS)
        read = reader(psi, t, z, rows)
        total = {}
        for chiral in range(2):
            vectors = []
            for column in range(6):
                real = read(2 * chiral + column // 3, 0, column % 3)
                imag = read(2 * chiral + column // 3, 1, column % 3)
                vectors.append((real, imag, real + imag))
            for row in range(6):
                spin, colour = 2 * chiral + row // 3, row % 3
                sums = None
                for column in range(6):
                    entry = three_rows(clover, t, z, (chiral * 6 + row) * 6 + column)
                    sums = products(entry, vectors[column], sums, False)
                real, imag = total_of(sums, False)
                total[(spin, 0, colour)] = vectors[row][0] + real
                total[(spin, 1, colour)] = vectors[row][1] + imag
        for direction in range(2):
            link = link_reader(links, t, z, direction)
            half = mapped(project(read, direction, -1), functools.partial(ahead, direction))
            spread(total, link_times(link, half, False), direction, -1)
            half = link_times(link, project(read, direction, 1), True)
            spread(total, mapped(half, functools.partial(behind, direction)), direction, 1)
        for key in KEYS:
            out[t, z, key[0], key[1], key[2], rows, :] = total[key]
        return carry

    lax.fori_loop(0, slices * layers * halves, plane, 0)

    def bonds(direction, count, low_cell, high_cell):
        def bond(i, carry):
            other = i // halves
            rows = pl.ds(pl.multiple_of((i % halves) * ROWS, ROWS), ROWS)
            low, high = low_cell(other), high_cell(other)
            link = link_reader(links, *low, direction)
            for source, target, adjoint in ((high, low, False), (low, high, True)):
                sign = 1 if adjoint else -1
                half = link_times(link, project(reader(psi, *source, rows), direction, sign), adjoint)
                read = reader(out, *target, rows)
                total = {key: read(*key) for key in KEYS}
                spread(total, half, direction, sign)
                for key in KEYS:
                    out[target[0], target[1], key[0], key[1], key[2], rows, :] = total[key]
            return carry

        lax.fori_loop(0, count * halves, bond, 0)

    for z in range(layers - 1):
        bonds(2, slices, lambda t, z=z: (t, z), lambda t, z=z: (t, z + 1))
    for t in range(slices - 1):
        bonds(3, layers, lambda z, t=t: (t, z), lambda z, t=t: (t + 1, z))


def half_value(ref, index):
    return [
        [[ref[index, s, r, c].astype(F32) for c in range(3)] for r in range(2)] for s in range(2)
    ]


def put_half(ref, index, half):
    for s in range(2):
        for r in range(2):
            for c in range(3):
                ref[index, s, r, c] = half[s][r][c].astype(BF16)


def by_parity(place, function, pair):
    odd = place % 2 == 1
    pl.when(odd)(lambda: function(pair[0], pair[1]))
    pl.when(jnp.logical_not(odd))(lambda: function(pair[1], pair[0]))


def faces_part(psi, links, where, t_outer, t_inner, z_outer, z_inner):
    by_parity(where[0], functools.partial(z_faces, psi, links), (z_inner, z_outer))
    by_parity(where[1], functools.partial(t_faces, psi, links), (t_inner, t_outer))


def z_faces(psi, links, z_low, z_high):
    slices, layers = psi.shape[0], psi.shape[1]
    rows = slice(None)

    def of_z(t, carry):
        put_half(z_low, t, project(reader(psi, t, 0, rows), 2, -1))
        half = project(reader(psi, t, layers - 1, rows), 2, 1)
        put_half(z_high, t, link_times(link_reader(links, t, layers - 1, 2), half, True))
        return carry

    lax.fori_loop(0, slices, of_z, 0)


def t_faces(psi, links, t_low, t_high):
    slices, layers = psi.shape[0], psi.shape[1]
    rows = slice(None)

    def of_t(z, carry):
        put_half(t_low, z, project(reader(psi, 0, z, rows), 3, -1))
        half = project(reader(psi, slices - 1, z, rows), 3, 1)
        put_half(t_high, z, link_times(link_reader(links, slices - 1, z, 3), half, True))
        return carry

    lax.fori_loop(0, layers, of_t, 0)


def put(source, out, target, half, direction, sign):
    t, z = target
    read = reader(source, t, z, slice(None))
    total = {key: read(*key) for key in KEYS}
    spread(total, half, direction, sign)
    for key in KEYS:
        out[t, z, key[0], key[1], key[2]] = total[key]


def halo_part(acc, links, where, t_outer, t_inner, z_outer, z_inner, out):
    by_parity(where[0], functools.partial(z_halo, acc, links, out), (z_inner, z_outer))
    by_parity(where[1], functools.partial(t_halo, links, where, out), (t_inner, t_outer))


def z_halo(acc, links, out, z_before, z_after):
    slices, layers = acc.shape[0], acc.shape[1]

    def of_z(t, carry):
        for z in range(1, layers - 1):
            for key in KEYS:
                out[t, z, key[0], key[1], key[2]] = acc[t, z, key[0], key[1], key[2]]
        put(acc, out, (t, 0), half_value(z_before, t), 2, 1)
        half = link_times(link_reader(links, t, layers - 1, 2), half_value(z_after, t), False)
        put(acc, out, (t, layers - 1), half, 2, -1)
        return carry

    lax.fori_loop(0, slices, of_z, 0)


def t_halo(links, where, out, t_before, t_after):
    slices, layers = out.shape[0], out.shape[1]
    first = jnp.where(where[1] == 0, -1.0, 1.0).astype(F32)
    last = jnp.where(where[1] == where[2] - 1, -1.0, 1.0).astype(F32)

    def of_t(z, carry):
        put(out, out, (0, z), mapped(half_value(t_before, z), lambda v: v * first), 3, 1)
        half = mapped(half_value(t_after, z), lambda v: v * last)
        half = link_times(link_reader(links, slices - 1, z, 3), half, False)
        put(out, out, (slices - 1, z), half, 3, -1)
        return carry

    lax.fori_loop(0, layers, of_t, 0)


def position():
    return lax.axis_index("space"), lax.axis_index("tm"), lax.axis_size("tm")


VMEM = pl.BlockSpec(memory_space=pltpu.VMEM)
FAR = pl.BlockSpec(memory_space=pltpu.HBM)


def in_far(value):
    return pltpu.with_memory_space_constraint(value, pltpu.HBM)


def call(kernel, in_count, out_shapes, scratch=(), far=(), flops=1 << 22, name=None):
    specs = [FAR if i in far else VMEM for i in range(in_count)]
    return pl.pallas_call(
        kernel,
        out_shape=out_shapes,
        in_specs=specs,
        out_specs=jax.tree.map(lambda _: VMEM, out_shapes),
        scratch_shapes=list(scratch),
        cost_estimate=pl.CostEstimate(flops=flops, bytes_accessed=1 << 21, transcendentals=0),
        compiler_params=pltpu.CompilerParams(vmem_limit_bytes=LIMIT),
        name=name,
    )


def entry_kernel(source_far, gauge_far, clover_far, psi, links, *refs):
    sent, (clover, source, gauge, arrived) = refs[:4], refs[4:]
    gauge_copy = pltpu.make_async_copy(gauge_far, gauge, arrived.at[0])
    source_copy = pltpu.make_async_copy(source_far, source, arrived.at[1])
    clover_copy = pltpu.make_async_copy(clover_far, clover, arrived.at[2])
    gauge_copy.start()
    source_copy.start()
    clover_copy.start()
    gauge_copy.wait()
    slices, layers = source.shape[0], source.shape[1]
    for t in range(slices):
        for z in range(layers):
            for mu in range(4):
                for a in range(3):
                    for b in range(3):
                        value = gauge[t, z, mu, a, b].astype(F32) * (-HOPPING)
                        put_three_rows(links, t, z, (mu * 3 + a) * 3 + b, value)
    source_copy.wait()
    psi[...] = source[...].astype(F32)
    faces_part(psi, links, position(), *sent)
    clover_copy.wait()


def clover_kernel(clover, rows):
    slices, layers = clover.shape[0], clover.shape[1]
    for t in range(slices):
        for z in range(layers):
            for chiral in range(2):
                for i in range(6):
                    for j in range(6):
                        value = clover[t, z, chiral, i, j].astype(F32)
                        put_three_rows(rows, t, z, (chiral * 6 + i) * 6 + j, value)


def local_kernel(psi, links, clover, out):
    local_part(psi, links, clover, out)


def middle_kernel(acc, links, *refs):
    received, (psi, *sent) = refs[:4], refs[4:]
    halo_part(acc, links, position(), *received, psi)
    faces_part(psi, links, position(), *sent)


def last_kernel(acc, links, *refs):
    received, (result, psi) = refs[:4], refs[4:]
    halo_part(acc, links, position(), *received, psi)
    result[...] = psi[...].astype(BF16)


def coefficient_kernel(scale, acc, links, *refs):
    received, (vectors, result, psi, rounded) = refs[:4], refs[4:]
    halo_part(acc, links, position(), *received, psi)
    slices, layers = acc.shape[0], acc.shape[1]
    columns = acc.shape[5]
    half_count = vectors.shape[4] // 128
    for t in range(slices):
        for z in range(layers):
            for colour in range(3):
                for spin in range(4):
                    for ri in range(2):
                        row = (ri * 4 + spin) * columns
                        rounded[t, z, colour, pl.ds(row, columns), :] = psi[
                            t, z, spin, ri, colour
                        ].astype(BF16)
    side = 4 * columns
    for t in range(slices):
        sums = []
        for part in range(2):
            total = None
            for z in range(layers):
                for colour in range(3):
                    product = lax.dot_general(
                        rounded[t, z, colour],
                        vectors[t, z, part, colour],
                        (((1,), (1,)), ((), ())),
                        preferred_element_type=F32,
                    )
                    total = product if total is None else total + product
            sums.append(total)
        real = (sums[0][:side] + sums[1][side:]) * scale
        imag = (sums[0][side:] - sums[1][:side]) * scale
        for ri, value in enumerate((real, imag)):
            for k in range(half_count):
                row = (t * 2 + ri) * half_count + k
                result[:, row, :] = value[:, k * 128 : (k + 1) * 128]


def mix_kernel(shares, elemental, result):
    slices = elemental.shape[0]
    eigen_count = elemental.shape[2]
    half_count = eigen_count // 128
    total = jnp.sum(shares[...], axis=0)

    def pieces(value):
        first = value.astype(BF16)
        rest = value - first.astype(F32)
        second = rest.astype(BF16)
        third = (rest - second.astype(F32)).astype(BF16)
        return [first, second, third]

    def row_of(t, ri):
        start = (t * 2 + ri) * half_count
        return jnp.concatenate([total[start + k : start + k + 1] for k in range(half_count)], axis=1)

    for t in range(slices):
        parts = jnp.concatenate([row_of(t, 0), row_of(t, 1)], axis=0)
        terms = []
        for component in range(2):
            weights = elemental[t, component]
            whole = None
            for piece in pieces(parts):
                product = lax.dot_general(
                    piece, weights, (((1,), (1,)), ((), ())), preferred_element_type=F32
                )
                whole = product if whole is None else whole + product
            terms.append(whole)
        real = terms[0][0:1] - terms[1][1:2]
        imag = terms[0][1:2] + terms[1][0:1]
        for ri, value in enumerate((real, imag)):
            for k in range(half_count):
                row = (t * 2 + ri) * half_count + k
                piece = value[:, k * 128 : (k + 1) * 128].astype(BF16)
                result[:, row : row + 1, :] = jnp.broadcast_to(
                    piece[None], (result.shape[0], 1, 128)
                )


def expand_kernel(mixed, vectors, links, psi, *refs):
    sent, (turned, left) = refs[:4], refs[4:]
    slices, layers = psi.shape[0], psi.shape[1]
    columns = psi.shape[5]
    eigen_count = vectors.shape[4]
    half_count = eigen_count // 128
    side = 4 * columns
    scale = eigen_count ** (-0.5)
    turned[...] = mixed[...].astype(F32)
    for t in range(slices):
        for ri in range(2):
            for k in range(half_count):
                row = (t * 2 + ri) * half_count + k
                value = turned[:, row, :]
                lanes = slice(k * 128, (k + 1) * 128)
                own = value.astype(BF16)
                if ri == 0:
                    left[0, :side, lanes] = own
                    left[1, side:, lanes] = own
                else:
                    left[0, side:, lanes] = own
                    left[1, :side, lanes] = (-value).astype(BF16)
        for z in range(layers):
            for colour in range(3):
                value = jnp.dot(left[0], vectors[t, z, 0, colour], preferred_element_type=F32)
                value += jnp.dot(left[1], vectors[t, z, 1, colour], preferred_element_type=F32)
                value = value * scale
                for ri in range(2):
                    for spin in range(4):
                        row = (ri * 4 + spin) * columns
                        psi[t, z, spin, ri, colour] = value[row : row + columns]
    faces_part(psi, links, position(), *sent)


def on_device(source, gauge_links, clover, eigenvectors, elemental):
    slices, layers = source.shape[0], source.shape[1]
    columns, sites = source.shape[5], source.shape[6]
    eigen_count = eigenvectors.shape[4]
    space_count = lax.axis_size("space")
    spinor_type = jax.ShapeDtypeStruct(source.shape, F32)
    z_face = jax.ShapeDtypeStruct((slices, 2, 2, 3, columns, sites), BF16)
    t_face = jax.ShapeDtypeStruct((layers, 2, 2, 3, columns, sites), BF16)
    faces = (t_face, t_face, z_face, z_face)
    link_rows = jax.ShapeDtypeStruct((slices, layers, 108, sites), F32)
    clover_rows = jax.ShapeDtypeStruct((slices, layers, 216, sites), F32)
    row_count = slices * 2 * eigen_count // 128

    def swapped(value, axis, offset):
        count = lax.axis_size(axis)
        pairs = [(i % count, (i + 1) % count) for i in range(offset, count + offset, 2)]
        return lax.ppermute(value, axis, pairs + [(b, a) for a, b in pairs])

    def exchanged(t_outer, t_inner, z_outer, z_inner):
        return (
            swapped(t_outer, "tm", 1),
            swapped(t_inner, "tm", 0),
            swapped(z_outer, "space", 1),
            swapped(z_inner, "space", 0),
        )

    gauge = jnp.transpose(gauge_links, (0, 1, 2, 4, 5, 3, 6))
    clover = jnp.transpose(clover, (0, 1, 2, 4, 5, 3, 6))
    clover_near = jax.ShapeDtypeStruct(clover.shape, BF16)
    psi, links, *sent, clover = call(
        entry_kernel,
        3,
        (spinor_type, link_rows) + faces + (clover_near,),
        scratch=(
            pltpu.VMEM(source.shape, BF16),
            pltpu.VMEM(gauge.shape, BF16),
            pltpu.SemaphoreType.DMA((3,)),
        ),
        far=(0, 1, 2),
        name="entry",
    )(in_far(source), in_far(gauge), in_far(clover))
    got = exchanged(*sent)
    clover_f32 = call(clover_kernel, 1, clover_rows, name="clover_rows")(clover)

    def local(spinor):
        return call(local_kernel, 3, spinor_type, flops=1 << 26, name="local")(
            spinor, links, clover_f32
        )

    def middle(acc, received):
        return call(middle_kernel, 6, (spinor_type,) + faces, name="middle")(
            acc, links, *received
        )

    acc = local(psi)
    psi, *sent = middle(acc, got)
    got = exchanged(*sent)
    acc = local(psi)
    normaliser = (3.0 * X * Y * layers * space_count) ** (-0.5)
    scratch_psi = pltpu.VMEM(source.shape, F32)
    partial_sums = call(
        functools.partial(coefficient_kernel, normaliser),
        7,
        jax.ShapeDtypeStruct((4 * columns, row_count, 128), F32),
        scratch=(scratch_psi, pltpu.VMEM((slices, layers, 3, 8 * columns, sites), BF16)),
        name="coefficients",
    )(acc, links, *got, eigenvectors)
    shares = lax.all_to_all(partial_sums, "space", 0, 0, tiled=True)
    mixed = call(
        mix_kernel,
        2,
        jax.ShapeDtypeStruct((space_count, row_count, 128), BF16),
        name="mix",
    )(shares, elemental)
    mixed = lax.all_to_all(mixed, "space", 0, 0, tiled=True)
    psi, *sent = call(
        expand_kernel,
        3,
        (spinor_type,) + faces,
        scratch=(
            pltpu.VMEM((4 * columns, row_count, 128), F32),
            pltpu.VMEM((2, 8 * columns, eigen_count), BF16),
        ),
        name="expand",
    )(mixed, eigenvectors, links)
    got = exchanged(*sent)
    acc = local(psi)
    psi, *sent = middle(acc, got)
    got = exchanged(*sent)
    acc = local(psi)
    return call(
        last_kernel,
        6,
        jax.ShapeDtypeStruct(source.shape, BF16),
        scratch=(scratch_psi,),
        name="last",
    )(acc, links, *got)


def solution(mesh):
    placed = (
        P("tm", "space", None, None, None, None, None),
        P("tm", "space", None, None, None, None, None),
        P("tm", "space", None, None, None, None, None),
        P("tm", "space", None, None, None, None),
        P("tm", None, None, None),
    )
    return jax.shard_map(
        on_device,
        mesh=mesh,
        in_specs=placed,
        out_specs=P("tm", "space", None, None, None, None, None),
        check_vma=False,
    )
```

```python
import functools

import jax
import jax.numpy as jnp
from jax import lax
from jax.experimental import pallas as pl
from jax.experimental.pallas import tpu as pltpu
from jax.sharding import PartitionSpec as P

X = 16
Y = 8

HOPPING = 0.125
HALF_MAP = (
    ((1, 0.0, -1.0), (0, 0.0, -1.0)),
    ((1, -1.0, 0.0), (0, 1.0, 0.0)),
    ((0, 0.0, -1.0), (1, 0.0, 1.0)),
    ((0, 1.0, 0.0), (1, 1.0, 0.0)),
)
ROWS = 16
LIMIT = 16 << 20
F32 = jnp.float32
BF16 = jnp.bfloat16


def dagger_map(forward_map):
    result = [None, None]
    for row_number in range(2):
        column, real_coef, imag_coef = forward_map[row_number]
        result[column] = (row_number, real_coef, -imag_coef)
    return tuple(result)


def plus(left, right, sign):
    return left + right if sign > 0 else left - right


def project(spinor, direction, sign):
    half = []
    for row, (column, a, b) in enumerate(HALF_MAP[direction]):
        real, imag = [], []
        for colour in range(3):
            if a != 0.0:
                real.append(plus(spinor(row, 0, colour), spinor(2 + column, 0, colour), sign * a))
                imag.append(plus(spinor(row, 1, colour), spinor(2 + column, 1, colour), sign * a))
            else:
                real.append(plus(spinor(row, 0, colour), spinor(2 + column, 1, colour), -sign * b))
                imag.append(plus(spinor(row, 1, colour), spinor(2 + column, 0, colour), sign * b))
        half.append([real, imag])
    return half


def products(rows, vector, sums, conjugate):
    real, less, more = rows
    vr, vi, both = vector
    terms = (real * both, more * vr, less * vi) if conjugate else (real * both, less * vr, more * vi)
    return list(terms) if sums is None else [old + new for old, new in zip(sums, terms)]


def total_of(sums, conjugate):
    if conjugate:
        return sums[0] + sums[2], sums[0] - sums[1]
    return sums[0] - sums[2], sums[0] + sums[1]


def link_times(link, half, adjoint):
    result = [[[None] * 3, [None] * 3] for _ in range(2)]
    vectors = [
        [(h[0][b], h[1][b], h[0][b] + h[1][b]) for b in range(3)] for h in half
    ]
    for a in range(3):
        sums = [None, None]
        for b in range(3):
            rows = link(b, a) if adjoint else link(a, b)
            for spin in range(2):
                sums[spin] = products(rows, vectors[spin][b], sums[spin], adjoint)
        for spin in range(2):
            result[spin][0][a], result[spin][1][a] = total_of(sums[spin], adjoint)
    return result


def lower_terms(half, direction):
    terms = []
    for row, (column, a, b) in enumerate(dagger_map(HALF_MAP[direction])):
        for colour in range(3):
            if a != 0.0:
                terms.append((2 + row, 0, colour, a, half[column][0][colour]))
                terms.append((2 + row, 1, colour, a, half[column][1][colour]))
            else:
                terms.append((2 + row, 0, colour, -b, half[column][1][colour]))
                terms.append((2 + row, 1, colour, b, half[column][0][colour]))
    return terms


def spread(total, half, direction, lower_sign):
    for spin in range(2):
        for ri in range(2):
            for colour in range(3):
                key = (spin, ri, colour)
                total[key] = total[key] + half[spin][ri][colour]
    for spin, ri, colour, sign, value in lower_terms(half, direction):
        key = (spin, ri, colour)
        total[key] = plus(total[key], value, sign * lower_sign)


def mapped(half, function):
    return [[[function(v) for v in part] for part in spin] for spin in half]


def reader(ref, t, z, rows):
    return lambda spin, ri, colour: ref[t, z, spin, ri, colour, rows, :].astype(F32)


def three_rows(ref, t, z, entry):
    return [ref[t, z, pl.ds(entry * 3 + i, 1), :] for i in range(3)]


def put_three_rows(ref, t, z, entry, value):
    real, imag = value[0:1], value[1:2]
    for i, row in enumerate((real, imag - real, imag + real)):
        ref[t, z, pl.ds(entry * 3 + i, 1), :] = row


def link_reader(links, t, z, mu):
    return lambda a, b: three_rows(links, t, z, (mu * 3 + a) * 3 + b)


KEYS = [(s, r, c) for s in range(4) for r in range(2) for c in range(3)]


def local_part(psi, links, clover, out):
    layers = psi.shape[1]
    slices = psi.shape[0]
    halves = psi.shape[5] // ROWS
    lane = lax.broadcasted_iota(jnp.int32, (ROWS, X * Y), 1) % X
    at_last = lane == X - 1
    at_first = lane == 0

    def ahead(direction, value):
        if direction == 1:
            return pltpu.roll(value, X * Y - X, 1)
        return jnp.where(at_last, pltpu.roll(value, X - 1, 1), pltpu.roll(value, X * Y - 1, 1))

    def behind(direction, value):
        if direction == 1:
            return pltpu.roll(value, X, 1)
        return jnp.where(at_first, pltpu.roll(value, X * Y - X + 1, 1), pltpu.roll(value, 1, 1))

    def plane(i, carry):
        t = i // (layers * halves)
        z = (i // halves) % layers
        rows = pl.ds(pl.multiple_of((i % halves) * ROWS, ROWS), ROWS)
        read = reader(psi, t, z, rows)
        total = {}
        for chiral in range(2):
            vectors = []
            for column in range(6):
                real = read(2 * chiral + column // 3, 0, column % 3)
                imag = read(2 * chiral + column // 3, 1, column % 3)
                vectors.append((real, imag, real + imag))
            for row in range(6):
                spin, colour = 2 * chiral + row // 3, row % 3
                sums = None
                for column in range(6):
                    entry = three_rows(clover, t, z, (chiral * 6 + row) * 6 + column)
                    sums = products(entry, vectors[column], sums, False)
                real, imag = total_of(sums, False)
                total[(spin, 0, colour)] = vectors[row][0] + real
                total[(spin, 1, colour)] = vectors[row][1] + imag
        for direction in range(2):
            link = link_reader(links, t, z, direction)
            half = mapped(project(read, direction, -1), functools.partial(ahead, direction))
            spread(total, link_times(link, half, False), direction, -1)
            half = link_times(link, project(read, direction, 1), True)
            spread(total, mapped(half, functools.partial(behind, direction)), direction, 1)
        for key in KEYS:
            out[t, z, key[0], key[1], key[2], rows, :] = total[key]
        return carry

    lax.fori_loop(0, slices * layers * halves, plane, 0)

    def bonds(direction, count, low_cell, high_cell):
        def bond(i, carry):
            other = i // halves
            rows = pl.ds(pl.multiple_of((i % halves) * ROWS, ROWS), ROWS)
            low, high = low_cell(other), high_cell(other)
            link = link_reader(links, *low, direction)
            for source, target, adjoint in ((high, low, False), (low, high, True)):
                sign = 1 if adjoint else -1
                half = link_times(link, project(reader(psi, *source, rows), direction, sign), adjoint)
                read = reader(out, *target, rows)
                total = {key: read(*key) for key in KEYS}
                spread(total, half, direction, sign)
                for key in KEYS:
                    out[target[0], target[1], key[0], key[1], key[2], rows, :] = total[key]
            return carry

        lax.fori_loop(0, count * halves, bond, 0)

    for z in range(layers - 1):
        bonds(2, slices, lambda t, z=z: (t, z), lambda t, z=z: (t, z + 1))
    for t in range(slices - 1):
        bonds(3, layers, lambda z, t=t: (t, z), lambda z, t=t: (t + 1, z))


def half_value(ref, index):
    return [
        [[ref[index, s, r, c].astype(F32) for c in range(3)] for r in range(2)] for s in range(2)
    ]


def put_half(ref, index, half):
    for s in range(2):
        for r in range(2):
            for c in range(3):
                ref[index, s, r, c] = half[s][r][c].astype(BF16)


def by_parity(place, function, pair):
    odd = place % 2 == 1
    pl.when(odd)(lambda: function(pair[0], pair[1]))
    pl.when(jnp.logical_not(odd))(lambda: function(pair[1], pair[0]))


def faces_part(psi, links, where, z_outer, z_inner, t_outer, t_inner):
    by_parity(where[0], functools.partial(z_faces, psi, links), (z_inner, z_outer))
    by_parity(where[1], functools.partial(t_faces, psi, links), (t_inner, t_outer))


def z_faces(psi, links, z_low, z_high):
    slices, layers = psi.shape[0], psi.shape[1]
    rows = slice(None)

    def of_z(t, carry):
        put_half(z_low, t, project(reader(psi, t, 0, rows), 2, -1))
        half = project(reader(psi, t, layers - 1, rows), 2, 1)
        put_half(z_high, t, link_times(link_reader(links, t, layers - 1, 2), half, True))
        return carry

    lax.fori_loop(0, slices, of_z, 0)


def t_faces(psi, links, t_low, t_high):
    slices, layers = psi.shape[0], psi.shape[1]
    rows = slice(None)

    def of_t(z, carry):
        put_half(t_low, z, project(reader(psi, 0, z, rows), 3, -1))
        half = project(reader(psi, slices - 1, z, rows), 3, 1)
        put_half(t_high, z, link_times(link_reader(links, slices - 1, z, 3), half, True))
        return carry

    lax.fori_loop(0, layers, of_t, 0)


def put(source, out, target, half, direction, sign):
    t, z = target
    read = reader(source, t, z, slice(None))
    total = {key: read(*key) for key in KEYS}
    spread(total, half, direction, sign)
    for key in KEYS:
        out[t, z, key[0], key[1], key[2]] = total[key]


def halo_part(acc, links, where, z_outer, z_inner, t_outer, t_inner, out):
    by_parity(where[0], functools.partial(z_halo, acc, links, out), (z_inner, z_outer))
    by_parity(where[1], functools.partial(t_halo, links, where, out), (t_inner, t_outer))


def z_halo(acc, links, out, z_before, z_after):
    slices, layers = acc.shape[0], acc.shape[1]

    def of_z(t, carry):
        for z in range(1, layers - 1):
            for key in KEYS:
                out[t, z, key[0], key[1], key[2]] = acc[t, z, key[0], key[1], key[2]]
        put(acc, out, (t, 0), half_value(z_before, t), 2, 1)
        half = link_times(link_reader(links, t, layers - 1, 2), half_value(z_after, t), False)
        put(acc, out, (t, layers - 1), half, 2, -1)
        return carry

    lax.fori_loop(0, slices, of_z, 0)


def t_halo(links, where, out, t_before, t_after):
    slices, layers = out.shape[0], out.shape[1]
    first = jnp.where(where[1] == 0, -1.0, 1.0).astype(F32)
    last = jnp.where(where[1] == where[2] - 1, -1.0, 1.0).astype(F32)

    def of_t(z, carry):
        put(out, out, (0, z), mapped(half_value(t_before, z), lambda v: v * first), 3, 1)
        half = mapped(half_value(t_after, z), lambda v: v * last)
        half = link_times(link_reader(links, slices - 1, z, 3), half, False)
        put(out, out, (slices - 1, z), half, 3, -1)
        return carry

    lax.fori_loop(0, layers, of_t, 0)


def position():
    return lax.axis_index("space"), lax.axis_index("tm"), lax.axis_size("tm")


VMEM = pl.BlockSpec(memory_space=pltpu.VMEM)
FAR = pl.BlockSpec(memory_space=pltpu.HBM)


def in_far(value):
    return pltpu.with_memory_space_constraint(value, pltpu.HBM)


def call(kernel, in_count, out_shapes, scratch=(), far=(), flops=1 << 22, name=None):
    specs = [FAR if i in far else VMEM for i in range(in_count)]
    return pl.pallas_call(
        kernel,
        out_shape=out_shapes,
        in_specs=specs,
        out_specs=jax.tree.map(lambda _: VMEM, out_shapes),
        scratch_shapes=list(scratch),
        cost_estimate=pl.CostEstimate(flops=flops, bytes_accessed=1 << 21, transcendentals=0),
        compiler_params=pltpu.CompilerParams(vmem_limit_bytes=LIMIT),
        name=name,
    )


def entry_kernel(source_far, gauge_far, clover_far, psi, links, *refs):
    sent, (clover, source, gauge, arrived) = refs[:4], refs[4:]
    gauge_copy = pltpu.make_async_copy(gauge_far, gauge, arrived.at[0])
    source_copy = pltpu.make_async_copy(source_far, source, arrived.at[1])
    clover_copy = pltpu.make_async_copy(clover_far, clover, arrived.at[2])
    gauge_copy.start()
    source_copy.start()
    clover_copy.start()
    gauge_copy.wait()
    slices, layers = source.shape[0], source.shape[1]
    for t in range(slices):
        for z in range(layers):
            for mu in range(4):
                for a in range(3):
                    for b in range(3):
                        value = gauge[t, z, mu, a, b].astype(F32) * (-HOPPING)
                        put_three_rows(links, t, z, (mu * 3 + a) * 3 + b, value)
    source_copy.wait()
    psi[...] = source[...].astype(F32)
    faces_part(psi, links, position(), *sent)
    clover_copy.wait()


def clover_kernel(clover, rows):
    slices, layers = clover.shape[0], clover.shape[1]
    for t in range(slices):
        for z in range(layers):
            for chiral in range(2):
                for i in range(6):
                    for j in range(6):
                        value = clover[t, z, chiral, i, j].astype(F32)
                        put_three_rows(rows, t, z, (chiral * 6 + i) * 6 + j, value)


def local_kernel(psi, links, clover, out):
    local_part(psi, links, clover, out)


def middle_kernel(acc, links, *refs):
    received, (psi, *sent) = refs[:4], refs[4:]
    halo_part(acc, links, position(), *received, psi)
    faces_part(psi, links, position(), *sent)


def last_kernel(acc, links, *refs):
    received, (result, psi) = refs[:4], refs[4:]
    halo_part(acc, links, position(), *received, psi)
    result[...] = psi[...].astype(BF16)


def coefficient_kernel(scale, acc, links, *refs):
    received, (vectors, result, psi, rounded) = refs[:4], refs[4:]
    halo_part(acc, links, position(), *received, psi)
    slices, layers = acc.shape[0], acc.shape[1]
    columns = acc.shape[5]
    half_count = vectors.shape[4] // 128
    for t in range(slices):
        for z in range(layers):
            for colour in range(3):
                for spin in range(4):
                    for ri in range(2):
                        row = (ri * 4 + spin) * columns
                        rounded[t, z, colour, pl.ds(row, columns), :] = psi[
                            t, z, spin, ri, colour
                        ].astype(BF16)
    side = 4 * columns
    for t in range(slices):
        sums = []
        for part in range(2):
            total = None
            for z in range(layers):
                for colour in range(3):
                    product = lax.dot_general(
                        rounded[t, z, colour],
                        vectors[t, z, part, colour],
                        (((1,), (1,)), ((), ())),
                        preferred_element_type=F32,
                    )
                    total = product if total is None else total + product
            sums.append(total)
        real = (sums[0][:side] + sums[1][side:]) * scale
        imag = (sums[0][side:] - sums[1][:side]) * scale
        for ri, value in enumerate((real, imag)):
            for k in range(half_count):
                row = (t * 2 + ri) * half_count + k
                result[:, row, :] = value[:, k * 128 : (k + 1) * 128]


def mix_kernel(shares, elemental, result):
    slices = elemental.shape[0]
    eigen_count = elemental.shape[2]
    half_count = eigen_count // 128
    total = jnp.sum(shares[...], axis=0)

    def pieces(value):
        first = value.astype(BF16)
        rest = value - first.astype(F32)
        second = rest.astype(BF16)
        third = (rest - second.astype(F32)).astype(BF16)
        return [first, second, third]

    def row_of(t, ri):
        start = (t * 2 + ri) * half_count
        return jnp.concatenate([total[start + k : start + k + 1] for k in range(half_count)], axis=1)

    for t in range(slices):
        parts = jnp.concatenate([row_of(t, 0), row_of(t, 1)], axis=0)
        terms = []
        for component in range(2):
            weights = elemental[t, component]
            whole = None
            for piece in pieces(parts):
                product = lax.dot_general(
                    piece, weights, (((1,), (1,)), ((), ())), preferred_element_type=F32
                )
                whole = product if whole is None else whole + product
            terms.append(whole)
        real = terms[0][0:1] - terms[1][1:2]
        imag = terms[0][1:2] + terms[1][0:1]
        for ri, value in enumerate((real, imag)):
            for k in range(half_count):
                row = (t * 2 + ri) * half_count + k
                piece = value[:, k * 128 : (k + 1) * 128].astype(BF16)
                result[:, row : row + 1, :] = jnp.broadcast_to(
                    piece[None], (result.shape[0], 1, 128)
                )


def expand_kernel(mixed, vectors, links, psi, *refs):
    sent, (turned, left) = refs[:4], refs[4:]
    slices, layers = psi.shape[0], psi.shape[1]
    columns = psi.shape[5]
    eigen_count = vectors.shape[4]
    half_count = eigen_count // 128
    side = 4 * columns
    scale = eigen_count ** (-0.5)
    turned[...] = mixed[...].astype(F32)
    for t in range(slices):
        for ri in range(2):
            for k in range(half_count):
                row = (t * 2 + ri) * half_count + k
                value = turned[:, row, :]
                lanes = slice(k * 128, (k + 1) * 128)
                own = value.astype(BF16)
                if ri == 0:
                    left[0, :side, lanes] = own
                    left[1, side:, lanes] = own
                else:
                    left[0, side:, lanes] = own
                    left[1, :side, lanes] = (-value).astype(BF16)
        for z in range(layers):
            for colour in range(3):
                value = jnp.dot(left[0], vectors[t, z, 0, colour], preferred_element_type=F32)
                value += jnp.dot(left[1], vectors[t, z, 1, colour], preferred_element_type=F32)
                value = value * scale
                for ri in range(2):
                    for spin in range(4):
                        row = (ri * 4 + spin) * columns
                        psi[t, z, spin, ri, colour] = value[row : row + columns]
    faces_part(psi, links, position(), *sent)


def on_device(source, gauge_links, clover, eigenvectors, elemental):
    slices, layers = source.shape[0], source.shape[1]
    columns, sites = source.shape[5], source.shape[6]
    eigen_count = eigenvectors.shape[4]
    space_count = lax.axis_size("space")
    spinor_type = jax.ShapeDtypeStruct(source.shape, F32)
    z_face = jax.ShapeDtypeStruct((slices, 2, 2, 3, columns, sites), BF16)
    t_face = jax.ShapeDtypeStruct((layers, 2, 2, 3, columns, sites), BF16)
    faces = (z_face, z_face, t_face, t_face)
    link_rows = jax.ShapeDtypeStruct((slices, layers, 108, sites), F32)
    clover_rows = jax.ShapeDtypeStruct((slices, layers, 216, sites), F32)
    row_count = slices * 2 * eigen_count // 128

    def swapped(value, axis, offset):
        count = lax.axis_size(axis)
        pairs = [(i % count, (i + 1) % count) for i in range(offset, count + offset, 2)]
        return lax.ppermute(value, axis, pairs + [(b, a) for a, b in pairs])

    def exchanged(z_outer, z_inner, t_outer, t_inner):
        return (
            swapped(z_outer, "space", 1),
            swapped(z_inner, "space", 0),
            swapped(t_outer, "tm", 1),
            swapped(t_inner, "tm", 0),
        )

    gauge = jnp.transpose(gauge_links, (0, 1, 2, 4, 5, 3, 6))
    clover = jnp.transpose(clover, (0, 1, 2, 4, 5, 3, 6))
    clover_near = jax.ShapeDtypeStruct(clover.shape, BF16)
    psi, links, *sent, clover = call(
        entry_kernel,
        3,
        (spinor_type, link_rows) + faces + (clover_near,),
        scratch=(
            pltpu.VMEM(source.shape, BF16),
            pltpu.VMEM(gauge.shape, BF16),
            pltpu.SemaphoreType.DMA((3,)),
        ),
        far=(0, 1, 2),
        name="entry",
    )(in_far(source), in_far(gauge), in_far(clover))
    got = exchanged(*sent)
    clover_f32 = call(clover_kernel, 1, clover_rows, name="clover_rows")(clover)

    def local(spinor):
        return call(local_kernel, 3, spinor_type, flops=1 << 26, name="local")(
            spinor, links, clover_f32
        )

    def middle(acc, received):
        return call(middle_kernel, 6, (spinor_type,) + faces, name="middle")(
            acc, links, *received
        )

    acc = local(psi)
    psi, *sent = middle(acc, got)
    got = exchanged(*sent)
    acc = local(psi)
    normaliser = (3.0 * X * Y * layers * space_count) ** (-0.5)
    scratch_psi = pltpu.VMEM(source.shape, F32)
    partial_sums = call(
        functools.partial(coefficient_kernel, normaliser),
        7,
        jax.ShapeDtypeStruct((4 * columns, row_count, 128), F32),
        scratch=(scratch_psi, pltpu.VMEM((slices, layers, 3, 8 * columns, sites), BF16)),
        name="coefficients",
    )(acc, links, *got, eigenvectors)
    shares = lax.all_to_all(partial_sums, "space", 0, 0, tiled=True)
    mixed = call(
        mix_kernel,
        2,
        jax.ShapeDtypeStruct((space_count, row_count, 128), BF16),
        name="mix",
    )(shares, elemental)
    mixed = lax.all_to_all(mixed, "space", 0, 0, tiled=True)
    psi, *sent = call(
        expand_kernel,
        3,
        (spinor_type,) + faces,
        scratch=(
            pltpu.VMEM((4 * columns, row_count, 128), F32),
            pltpu.VMEM((2, 8 * columns, eigen_count), BF16),
        ),
        name="expand",
    )(mixed, eigenvectors, links)
    got = exchanged(*sent)
    acc = local(psi)
    psi, *sent = middle(acc, got)
    got = exchanged(*sent)
    acc = local(psi)
    return call(
        last_kernel,
        6,
        jax.ShapeDtypeStruct(source.shape, BF16),
        scratch=(scratch_psi,),
        name="last",
    )(acc, links, *got)


def solution(mesh):
    placed = (
        P("tm", "space", None, None, None, None, None),
        P("tm", "space", None, None, None, None, None),
        P("tm", "space", None, None, None, None, None),
        P("tm", "space", None, None, None, None),
        P("tm", None, None, None),
    )
    return jax.shard_map(
        on_device,
        mesh=mesh,
        in_specs=placed,
        out_specs=P("tm", "space", None, None, None, None, None),
        check_vma=False,
    )
```

```python
import functools

import jax
import jax.numpy as jnp
from jax import lax
from jax.experimental import pallas as pl
from jax.experimental.pallas import tpu as pltpu
from jax.sharding import PartitionSpec as P

X = 16
Y = 8

HOPPING = 0.125
HALF_MAP = (
    ((1, 0.0, -1.0), (0, 0.0, -1.0)),
    ((1, -1.0, 0.0), (0, 1.0, 0.0)),
    ((0, 0.0, -1.0), (1, 0.0, 1.0)),
    ((0, 1.0, 0.0), (1, 1.0, 0.0)),
)
ROWS = 16
LIMIT = 16 << 20
F32 = jnp.float32
BF16 = jnp.bfloat16


def dagger_map(forward_map):
    result = [None, None]
    for row_number in range(2):
        column, real_coef, imag_coef = forward_map[row_number]
        result[column] = (row_number, real_coef, -imag_coef)
    return tuple(result)


def plus(left, right, sign):
    return left + right if sign > 0 else left - right


def project(spinor, direction, sign):
    half = []
    for row, (column, a, b) in enumerate(HALF_MAP[direction]):
        real, imag = [], []
        for colour in range(3):
            if a != 0.0:
                real.append(plus(spinor(row, 0, colour), spinor(2 + column, 0, colour), sign * a))
                imag.append(plus(spinor(row, 1, colour), spinor(2 + column, 1, colour), sign * a))
            else:
                real.append(plus(spinor(row, 0, colour), spinor(2 + column, 1, colour), -sign * b))
                imag.append(plus(spinor(row, 1, colour), spinor(2 + column, 0, colour), sign * b))
        half.append([real, imag])
    return half


def products(rows, vector, sums, conjugate):
    real, less, more = rows
    vr, vi, both = vector
    terms = (real * both, more * vr, less * vi) if conjugate else (real * both, less * vr, more * vi)
    return list(terms) if sums is None else [old + new for old, new in zip(sums, terms)]


def total_of(sums, conjugate):
    if conjugate:
        return sums[0] + sums[2], sums[0] - sums[1]
    return sums[0] - sums[2], sums[0] + sums[1]


def link_times(link, half, adjoint):
    result = [[[None] * 3, [None] * 3] for _ in range(2)]
    vectors = [
        [(h[0][b], h[1][b], h[0][b] + h[1][b]) for b in range(3)] for h in half
    ]
    for a in range(3):
        sums = [None, None]
        for b in range(3):
            rows = link(b, a) if adjoint else link(a, b)
            for spin in range(2):
                sums[spin] = products(rows, vectors[spin][b], sums[spin], adjoint)
        for spin in range(2):
            result[spin][0][a], result[spin][1][a] = total_of(sums[spin], adjoint)
    return result


def lower_terms(half, direction):
    terms = []
    for row, (column, a, b) in enumerate(dagger_map(HALF_MAP[direction])):
        for colour in range(3):
            if a != 0.0:
                terms.append((2 + row, 0, colour, a, half[column][0][colour]))
                terms.append((2 + row, 1, colour, a, half[column][1][colour]))
            else:
                terms.append((2 + row, 0, colour, -b, half[column][1][colour]))
                terms.append((2 + row, 1, colour, b, half[column][0][colour]))
    return terms


def spread(total, half, direction, lower_sign):
    for spin in range(2):
        for ri in range(2):
            for colour in range(3):
                key = (spin, ri, colour)
                total[key] = total[key] + half[spin][ri][colour]
    for spin, ri, colour, sign, value in lower_terms(half, direction):
        key = (spin, ri, colour)
        total[key] = plus(total[key], value, sign * lower_sign)


def mapped(half, function):
    return [[[function(v) for v in part] for part in spin] for spin in half]


def reader(ref, t, z, rows):
    return lambda spin, ri, colour: ref[t, z, spin, ri, colour, rows, :].astype(F32)


def three_rows(ref, t, z, entry):
    return [ref[t, z, pl.ds(entry * 3 + i, 1), :] for i in range(3)]


def put_three_rows(ref, t, z, entry, value):
    real, imag = value[0:1], value[1:2]
    for i, row in enumerate((real, imag - real, imag + real)):
        ref[t, z, pl.ds(entry * 3 + i, 1), :] = row


def link_reader(links, t, z, mu):
    return lambda a, b: three_rows(links, t, z, (mu * 3 + a) * 3 + b)


KEYS = [(s, r, c) for s in range(4) for r in range(2) for c in range(3)]


def local_part(psi, links, clover, out):
    layers = psi.shape[1]
    slices = psi.shape[0]
    halves = psi.shape[5] // ROWS
    lane = lax.broadcasted_iota(jnp.int32, (ROWS, X * Y), 1) % X
    at_last = lane == X - 1
    at_first = lane == 0

    def ahead(direction, value):
        if direction == 1:
            return pltpu.roll(value, X * Y - X, 1)
        return jnp.where(at_last, pltpu.roll(value, X - 1, 1), pltpu.roll(value, X * Y - 1, 1))

    def behind(direction, value):
        if direction == 1:
            return pltpu.roll(value, X, 1)
        return jnp.where(at_first, pltpu.roll(value, X * Y - X + 1, 1), pltpu.roll(value, 1, 1))

    def plane(i, carry):
        t = i // (layers * halves)
        z = (i // halves) % layers
        rows = pl.ds(pl.multiple_of((i % halves) * ROWS, ROWS), ROWS)
        read = reader(psi, t, z, rows)
        total = {}
        for chiral in range(2):
            vectors = []
            for column in range(6):
                real = read(2 * chiral + column // 3, 0, column % 3)
                imag = read(2 * chiral + column // 3, 1, column % 3)
                vectors.append((real, imag, real + imag))
            for row in range(6):
                spin, colour = 2 * chiral + row // 3, row % 3
                sums = None
                for column in range(6):
                    entry = three_rows(clover, t, z, (chiral * 6 + row) * 6 + column)
                    sums = products(entry, vectors[column], sums, False)
                real, imag = total_of(sums, False)
                total[(spin, 0, colour)] = vectors[row][0] + real
                total[(spin, 1, colour)] = vectors[row][1] + imag
        for direction in range(2):
            link = link_reader(links, t, z, direction)
            half = mapped(project(read, direction, -1), functools.partial(ahead, direction))
            spread(total, link_times(link, half, False), direction, -1)
            half = link_times(link, project(read, direction, 1), True)
            spread(total, mapped(half, functools.partial(behind, direction)), direction, 1)
        for key in KEYS:
            out[t, z, key[0], key[1], key[2], rows, :] = total[key]
        return carry

    lax.fori_loop(0, slices * layers * halves, plane, 0)

    def bonds(direction, count, low_cell, high_cell):
        def bond(i, carry):
            other = i // halves
            rows = pl.ds(pl.multiple_of((i % halves) * ROWS, ROWS), ROWS)
            low, high = low_cell(other), high_cell(other)
            link = link_reader(links, *low, direction)
            for source, target, adjoint in ((high, low, False), (low, high, True)):
                sign = 1 if adjoint else -1
                half = link_times(link, project(reader(psi, *source, rows), direction, sign), adjoint)
                read = reader(out, *target, rows)
                total = {key: read(*key) for key in KEYS}
                spread(total, half, direction, sign)
                for key in KEYS:
                    out[target[0], target[1], key[0], key[1], key[2], rows, :] = total[key]
            return carry

        lax.fori_loop(0, count * halves, bond, 0)

    for z in range(layers - 1):
        bonds(2, slices, lambda t, z=z: (t, z), lambda t, z=z: (t, z + 1))
    for t in range(slices - 1):
        bonds(3, layers, lambda z, t=t: (t, z), lambda z, t=t: (t + 1, z))


def half_value(ref, index):
    return [
        [[ref[index, s, r, c].astype(F32) for c in range(3)] for r in range(2)] for s in range(2)
    ]


def put_half(ref, index, half):
    for s in range(2):
        for r in range(2):
            for c in range(3):
                ref[index, s, r, c] = half[s][r][c].astype(BF16)


def by_parity(place, function, pair):
    odd = place % 2 == 1
    pl.when(odd)(lambda: function(pair[0], pair[1]))
    pl.when(jnp.logical_not(odd))(lambda: function(pair[1], pair[0]))


def faces_part(psi, links, where, z_outer, t_outer, z_inner, t_inner):
    by_parity(where[0], functools.partial(z_faces, psi, links), (z_inner, z_outer))
    by_parity(where[1], functools.partial(t_faces, psi, links), (t_inner, t_outer))


def z_faces(psi, links, z_low, z_high):
    slices, layers = psi.shape[0], psi.shape[1]
    rows = slice(None)

    def of_z(t, carry):
        put_half(z_low, t, project(reader(psi, t, 0, rows), 2, -1))
        half = project(reader(psi, t, layers - 1, rows), 2, 1)
        put_half(z_high, t, link_times(link_reader(links, t, layers - 1, 2), half, True))
        return carry

    lax.fori_loop(0, slices, of_z, 0)


def t_faces(psi, links, t_low, t_high):
    slices, layers = psi.shape[0], psi.shape[1]
    rows = slice(None)

    def of_t(z, carry):
        put_half(t_low, z, project(reader(psi, 0, z, rows), 3, -1))
        half = project(reader(psi, slices - 1, z, rows), 3, 1)
        put_half(t_high, z, link_times(link_reader(links, slices - 1, z, 3), half, True))
        return carry

    lax.fori_loop(0, layers, of_t, 0)


def put(source, out, target, half, direction, sign):
    t, z = target
    read = reader(source, t, z, slice(None))
    total = {key: read(*key) for key in KEYS}
    spread(total, half, direction, sign)
    for key in KEYS:
        out[t, z, key[0], key[1], key[2]] = total[key]


def halo_part(acc, links, where, z_outer, t_outer, z_inner, t_inner, out):
    by_parity(where[0], functools.partial(z_halo, acc, links, out), (z_inner, z_outer))
    by_parity(where[1], functools.partial(t_halo, links, where, out), (t_inner, t_outer))


def z_halo(acc, links, out, z_before, z_after):
    slices, layers = acc.shape[0], acc.shape[1]

    def of_z(t, carry):
        for z in range(1, layers - 1):
            for key in KEYS:
                out[t, z, key[0], key[1], key[2]] = acc[t, z, key[0], key[1], key[2]]
        put(acc, out, (t, 0), half_value(z_before, t), 2, 1)
        half = link_times(link_reader(links, t, layers - 1, 2), half_value(z_after, t), False)
        put(acc, out, (t, layers - 1), half, 2, -1)
        return carry

    lax.fori_loop(0, slices, of_z, 0)


def t_halo(links, where, out, t_before, t_after):
    slices, layers = out.shape[0], out.shape[1]
    first = jnp.where(where[1] == 0, -1.0, 1.0).astype(F32)
    last = jnp.where(where[1] == where[2] - 1, -1.0, 1.0).astype(F32)

    def of_t(z, carry):
        put(out, out, (0, z), mapped(half_value(t_before, z), lambda v: v * first), 3, 1)
        half = mapped(half_value(t_after, z), lambda v: v * last)
        half = link_times(link_reader(links, slices - 1, z, 3), half, False)
        put(out, out, (slices - 1, z), half, 3, -1)
        return carry

    lax.fori_loop(0, layers, of_t, 0)


def position():
    return lax.axis_index("space"), lax.axis_index("tm"), lax.axis_size("tm")


VMEM = pl.BlockSpec(memory_space=pltpu.VMEM)
FAR = pl.BlockSpec(memory_space=pltpu.HBM)


def in_far(value):
    return pltpu.with_memory_space_constraint(value, pltpu.HBM)


def call(kernel, in_count, out_shapes, scratch=(), far=(), flops=1 << 22, name=None):
    specs = [FAR if i in far else VMEM for i in range(in_count)]
    return pl.pallas_call(
        kernel,
        out_shape=out_shapes,
        in_specs=specs,
        out_specs=jax.tree.map(lambda _: VMEM, out_shapes),
        scratch_shapes=list(scratch),
        cost_estimate=pl.CostEstimate(flops=flops, bytes_accessed=1 << 21, transcendentals=0),
        compiler_params=pltpu.CompilerParams(vmem_limit_bytes=LIMIT),
        name=name,
    )


def entry_kernel(source_far, gauge_far, clover_far, psi, links, *refs):
    sent, (clover, source, gauge, arrived) = refs[:4], refs[4:]
    gauge_copy = pltpu.make_async_copy(gauge_far, gauge, arrived.at[0])
    source_copy = pltpu.make_async_copy(source_far, source, arrived.at[1])
    clover_copy = pltpu.make_async_copy(clover_far, clover, arrived.at[2])
    gauge_copy.start()
    source_copy.start()
    clover_copy.start()
    gauge_copy.wait()
    slices, layers = source.shape[0], source.shape[1]
    for t in range(slices):
        for z in range(layers):
            for mu in range(4):
                for a in range(3):
                    for b in range(3):
                        value = gauge[t, z, mu, a, b].astype(F32) * (-HOPPING)
                        put_three_rows(links, t, z, (mu * 3 + a) * 3 + b, value)
    source_copy.wait()
    psi[...] = source[...].astype(F32)
    faces_part(psi, links, position(), *sent)
    clover_copy.wait()


def clover_kernel(clover, rows):
    slices, layers = clover.shape[0], clover.shape[1]
    for t in range(slices):
        for z in range(layers):
            for chiral in range(2):
                for i in range(6):
                    for j in range(6):
                        value = clover[t, z, chiral, i, j].astype(F32)
                        put_three_rows(rows, t, z, (chiral * 6 + i) * 6 + j, value)


def local_kernel(psi, links, clover, out):
    local_part(psi, links, clover, out)


def middle_kernel(acc, links, *refs):
    received, (psi, *sent) = refs[:4], refs[4:]
    halo_part(acc, links, position(), *received, psi)
    faces_part(psi, links, position(), *sent)


def last_kernel(acc, links, *refs):
    received, (result, psi) = refs[:4], refs[4:]
    halo_part(acc, links, position(), *received, psi)
    result[...] = psi[...].astype(BF16)


def coefficient_kernel(scale, acc, links, *refs):
    received, (vectors, result, psi, rounded) = refs[:4], refs[4:]
    halo_part(acc, links, position(), *received, psi)
    slices, layers = acc.shape[0], acc.shape[1]
    columns = acc.shape[5]
    half_count = vectors.shape[4] // 128
    for t in range(slices):
        for z in range(layers):
            for colour in range(3):
                for spin in range(4):
                    for ri in range(2):
                        row = (ri * 4 + spin) * columns
                        rounded[t, z, colour, pl.ds(row, columns), :] = psi[
                            t, z, spin, ri, colour
                        ].astype(BF16)
    side = 4 * columns
    for t in range(slices):
        sums = []
        for part in range(2):
            total = None
            for z in range(layers):
                for colour in range(3):
                    product = lax.dot_general(
                        rounded[t, z, colour],
                        vectors[t, z, part, colour],
                        (((1,), (1,)), ((), ())),
                        preferred_element_type=F32,
                    )
                    total = product if total is None else total + product
            sums.append(total)
        real = (sums[0][:side] + sums[1][side:]) * scale
        imag = (sums[0][side:] - sums[1][:side]) * scale
        for ri, value in enumerate((real, imag)):
            for k in range(half_count):
                row = (t * 2 + ri) * half_count + k
                result[:, row, :] = value[:, k * 128 : (k + 1) * 128]


def mix_kernel(shares, elemental, result):
    slices = elemental.shape[0]
    eigen_count = elemental.shape[2]
    half_count = eigen_count // 128
    total = jnp.sum(shares[...], axis=0)

    def pieces(value):
        first = value.astype(BF16)
        rest = value - first.astype(F32)
        second = rest.astype(BF16)
        third = (rest - second.astype(F32)).astype(BF16)
        return [first, second, third]

    def row_of(t, ri):
        start = (t * 2 + ri) * half_count
        return jnp.concatenate([total[start + k : start + k + 1] for k in range(half_count)], axis=1)

    for t in range(slices):
        parts = jnp.concatenate([row_of(t, 0), row_of(t, 1)], axis=0)
        terms = []
        for component in range(2):
            weights = elemental[t, component]
            whole = None
            for piece in pieces(parts):
                product = lax.dot_general(
                    piece, weights, (((1,), (1,)), ((), ())), preferred_element_type=F32
                )
                whole = product if whole is None else whole + product
            terms.append(whole)
        real = terms[0][0:1] - terms[1][1:2]
        imag = terms[0][1:2] + terms[1][0:1]
        for ri, value in enumerate((real, imag)):
            for k in range(half_count):
                row = (t * 2 + ri) * half_count + k
                piece = value[:, k * 128 : (k + 1) * 128].astype(BF16)
                result[:, row : row + 1, :] = jnp.broadcast_to(
                    piece[None], (result.shape[0], 1, 128)
                )


def expand_kernel(mixed, vectors, links, psi, *refs):
    sent, (turned, left) = refs[:4], refs[4:]
    slices, layers = psi.shape[0], psi.shape[1]
    columns = psi.shape[5]
    eigen_count = vectors.shape[4]
    half_count = eigen_count // 128
    side = 4 * columns
    scale = eigen_count ** (-0.5)
    turned[...] = mixed[...].astype(F32)
    for t in range(slices):
        for ri in range(2):
            for k in range(half_count):
                row = (t * 2 + ri) * half_count + k
                value = turned[:, row, :]
                lanes = slice(k * 128, (k + 1) * 128)
                own = value.astype(BF16)
                if ri == 0:
                    left[0, :side, lanes] = own
                    left[1, side:, lanes] = own
                else:
                    left[0, side:, lanes] = own
                    left[1, :side, lanes] = (-value).astype(BF16)
        for z in range(layers):
            for colour in range(3):
                value = jnp.dot(left[0], vectors[t, z, 0, colour], preferred_element_type=F32)
                value += jnp.dot(left[1], vectors[t, z, 1, colour], preferred_element_type=F32)
                value = value * scale
                for ri in range(2):
                    for spin in range(4):
                        row = (ri * 4 + spin) * columns
                        psi[t, z, spin, ri, colour] = value[row : row + columns]
    faces_part(psi, links, position(), *sent)


def on_device(source, gauge_links, clover, eigenvectors, elemental):
    slices, layers = source.shape[0], source.shape[1]
    columns, sites = source.shape[5], source.shape[6]
    eigen_count = eigenvectors.shape[4]
    space_count = lax.axis_size("space")
    spinor_type = jax.ShapeDtypeStruct(source.shape, F32)
    z_face = jax.ShapeDtypeStruct((slices, 2, 2, 3, columns, sites), BF16)
    t_face = jax.ShapeDtypeStruct((layers, 2, 2, 3, columns, sites), BF16)
    faces = (z_face, t_face, z_face, t_face)
    link_rows = jax.ShapeDtypeStruct((slices, layers, 108, sites), F32)
    clover_rows = jax.ShapeDtypeStruct((slices, layers, 216, sites), F32)
    row_count = slices * 2 * eigen_count // 128

    def swapped(value, axis, offset):
        count = lax.axis_size(axis)
        pairs = [(i % count, (i + 1) % count) for i in range(offset, count + offset, 2)]
        return lax.ppermute(value, axis, pairs + [(b, a) for a, b in pairs])

    def exchanged(z_outer, t_outer, z_inner, t_inner):
        return (
            swapped(z_outer, "space", 1),
            swapped(t_outer, "tm", 1),
            swapped(z_inner, "space", 0),
            swapped(t_inner, "tm", 0),
        )

    gauge = jnp.transpose(gauge_links, (0, 1, 2, 4, 5, 3, 6))
    clover = jnp.transpose(clover, (0, 1, 2, 4, 5, 3, 6))
    clover_near = jax.ShapeDtypeStruct(clover.shape, BF16)
    psi, links, *sent, clover = call(
        entry_kernel,
        3,
        (spinor_type, link_rows) + faces + (clover_near,),
        scratch=(
            pltpu.VMEM(source.shape, BF16),
            pltpu.VMEM(gauge.shape, BF16),
            pltpu.SemaphoreType.DMA((3,)),
        ),
        far=(0, 1, 2),
        name="entry",
    )(in_far(source), in_far(gauge), in_far(clover))
    got = exchanged(*sent)
    clover_f32 = call(clover_kernel, 1, clover_rows, name="clover_rows")(clover)

    def local(spinor):
        return call(local_kernel, 3, spinor_type, flops=1 << 26, name="local")(
            spinor, links, clover_f32
        )

    def middle(acc, received):
        return call(middle_kernel, 6, (spinor_type,) + faces, name="middle")(
            acc, links, *received
        )

    acc = local(psi)
    psi, *sent = middle(acc, got)
    got = exchanged(*sent)
    acc = local(psi)
    normaliser = (3.0 * X * Y * layers * space_count) ** (-0.5)
    scratch_psi = pltpu.VMEM(source.shape, F32)
    partial_sums = call(
        functools.partial(coefficient_kernel, normaliser),
        7,
        jax.ShapeDtypeStruct((4 * columns, row_count, 128), F32),
        scratch=(scratch_psi, pltpu.VMEM((slices, layers, 3, 8 * columns, sites), BF16)),
        name="coefficients",
    )(acc, links, *got, eigenvectors)
    shares = lax.all_to_all(partial_sums, "space", 0, 0, tiled=True)
    mixed = call(
        mix_kernel,
        2,
        jax.ShapeDtypeStruct((space_count, row_count, 128), BF16),
        name="mix",
    )(shares, elemental)
    mixed = lax.all_to_all(mixed, "space", 0, 0, tiled=True)
    psi, *sent = call(
        expand_kernel,
        3,
        (spinor_type,) + faces,
        scratch=(
            pltpu.VMEM((4 * columns, row_count, 128), F32),
            pltpu.VMEM((2, 8 * columns, eigen_count), BF16),
        ),
        name="expand",
    )(mixed, eigenvectors, links)
    got = exchanged(*sent)
    acc = local(psi)
    psi, *sent = middle(acc, got)
    got = exchanged(*sent)
    acc = local(psi)
    return call(
        last_kernel,
        6,
        jax.ShapeDtypeStruct(source.shape, BF16),
        scratch=(scratch_psi,),
        name="last",
    )(acc, links, *got)


def solution(mesh):
    placed = (
        P("tm", "space", None, None, None, None, None),
        P("tm", "space", None, None, None, None, None),
        P("tm", "space", None, None, None, None, None),
        P("tm", "space", None, None, None, None),
        P("tm", None, None, None),
    )
    return jax.shard_map(
        on_device,
        mesh=mesh,
        in_specs=placed,
        out_specs=P("tm", "space", None, None, None, None, None),
        check_vma=False,
    )
```
